128 devices in a mesh: rep: 32 (over y, z, core), feat: 4 (over x).
Axes of the slice: x: 4, y: 4, z: 4, core: 2. Of those that a mesh axis runs over, the one named last changes fastest.
Arguments:
- activations: bfloat16 [32768, 8192], P('rep', 'feat'), may hold values from -6 to 6
- out_grad: bfloat16 [32768, 512], P(('rep', 'feat')), may hold values from -6 to 6
- weight: float32 [8192, 512], P('feat'), may hold values from -0.25 to 0.25
- momentum: float32 [32, 8192, 512], P('rep', 'feat'), may hold values from -4 to 4
- select: int32 [32, 32], replicated, may hold values from 0 to 4095, as said below
Outputs:
- input_grad: float32 [32768, 8192], P('rep', 'feat')
- residual: float32 [32, 8192, 512], P('rep', 'feat')
- new_weight: float32 [8192, 512], P('feat')
The draws below stay inside these ranges and needn't reach their ends.
Inputs may be any that keep to these rules, and one draw needn't show every extreme that they name: `select`: each replica's row holds 32 distinct frequency rows.
All inputs are finite; a program needn't handle non-finite values.
Results may differ from the reference program's by a relative error of at most 0.0003.
Values may be sent and summed in bfloat16 or wider, within the bound.
A program may use at most 128 MiB of HBM per device.

```python
import jax
import jax.numpy as jnp
from jax import lax

D = 8192
KV = 512
CH = 64
K = 32
TOK = 1024
REPS = 32
TOKENS = 32768


def draw_select(key, part):

    def one_row(replica):
        order = jax.random.permutation(jax.random.fold_in(key, replica + 17), CH * CH)
        return order[:K]
    return jax.vmap(one_row)(jnp.arange(REPS)).astype(jnp.int32)


def steps_of(key, extent, split, smallest, high):
    factor_of = 1.0
    for position, blocks in split:
        heights = jax.random.uniform(jax.random.fold_in(jax.random.fold_in(key, 6), position), (blocks,), jnp.float32, smallest / len(split), high / len(split))
        factor_of = factor_of * jnp.repeat(jnp.exp(heights), extent[position] // blocks).reshape((-1,) + (1,) * (len(extent) - 1 - position))
    return factor_of


def gaussian(stream_key, dims, width, reach, pieces=(), held_as=jnp.bfloat16):
    entries = jax.random.normal(stream_key, dims, jnp.float32) * width
    if len(pieces) > 0:
        entries = steps_of(stream_key, dims, pieces, -0.22, 0.18) * entries
    return jnp.clip(entries, min=-reach, max=reach).astype(held_as)


def setup_inputs(seed: int = 0) -> dict:
    key_of = jax.random.split(jax.random.key(seed), 6)
    return {
        "activations": gaussian(key_of[0], (TOKENS, D), 1.0, 6.0, ((0, 32), (1, 4))),
        "out_grad": gaussian(key_of[1], (TOKENS, KV), 1.0, 6.0, ((0, 128),)),
        "weight": gaussian(key_of[2], (D, KV), KV ** -0.5, 0.25, ((0, 4),), jnp.float32),
        "momentum": gaussian(key_of[3], (REPS, D, KV), 0.5, 4.0, ((0, 32), (1, 4)), jnp.float32),
        "select": draw_select(jax.random.fold_in(key_of[5], 71), 0),
    }


momentum_decay = 0.9
step_rate = 0.5

def dct_table():
    index = jnp.arange(CH).astype(jnp.float32)
    table = jnp.cos(jnp.pi * (2.0 * index[None, :] + 1.0) * index[:, None] / (2.0 * CH)) * jnp.sqrt(2.0 / CH)
    first = jnp.where(jnp.arange(CH) == 0, jnp.sqrt(0.5), 1.0).astype(jnp.float32)
    return table * first[:, None]

def forward(field, table):
    blocks = field.reshape(field.shape[0] // CH, CH, field.shape[1] // CH, CH)
    inner = jnp.einsum('iajb,vb->iajv', blocks, table, precision=lax.Precision.HIGHEST)
    coef = jnp.einsum('ua,iajv->uvij', table, inner, precision=lax.Precision.HIGHEST)
    return coef.reshape(CH * CH, -1)

def inverse(coef, nrows, ncols, table):
    blocks = coef.reshape(CH, CH, nrows // CH, ncols // CH)
    inner = jnp.einsum('uvij,vb->uijb', blocks, table, precision=lax.Precision.HIGHEST)
    field = jnp.einsum('ua,uijb->iajb', table, inner, precision=lax.Precision.HIGHEST)
    return field.reshape(nrows, ncols)

def reference(activations, out_grad, weight, momentum, select):
    table = dct_table()

    def one_replica(total, replica):
        x_rows = lax.dynamic_slice_in_dim(activations, replica * TOK, TOK, 0)
        g_rows = lax.dynamic_slice_in_dim(out_grad, replica * TOK, TOK, 0)
        in_grad = jnp.dot(g_rows.astype(jnp.float32), weight.T, precision=lax.Precision.HIGHEST)
        grad = jnp.dot(x_rows.T, g_rows, preferred_element_type=jnp.float32) / TOK
        moment = momentum_decay * momentum[replica] + grad
        coef = forward(moment, table)
        rows = select[replica]
        kept = jnp.zeros_like(coef).at[rows].set(coef[rows])
        back = inverse(kept, D, KV, table)
        return (total + back, (in_grad, moment - back))
    total, (grads, residual) = lax.scan(one_replica, jnp.zeros((D, KV), jnp.float32), jnp.arange(REPS).astype(jnp.int32))
    new_weight = weight - step_rate * total
    return (grads.reshape(REPS * TOK, D), residual, new_weight)
```

```python
import functools

import jax
import jax.numpy as jnp
from jax import lax
from jax.experimental import pallas as pl
from jax.experimental.pallas import tpu as pltpu
from jax.sharding import PartitionSpec as P

CH = 64
MOMENTUM_DECAY = 0.9
STEP_RATE = 0.5
f32 = jnp.float32
bf16 = jnp.bfloat16
NN = (((1,), (0,)), ((), ()))
NT = (((1,), (1,)), ((), ()))
TN = (((0,), (0,)), ((), ()))
MIB = 1 << 20


def dot(a, b, dims, precision=None):
    return lax.dot_general(a, b, dims, precision=precision, preferred_element_type=f32)


def split(v):
    high = v.astype(bf16)
    return high, (v - high.astype(f32)).astype(bf16)


def dct_transposed():
    a = lax.broadcasted_iota(jnp.int32, (CH, CH), 0)
    u = lax.broadcasted_iota(jnp.int32, (CH, CH), 1)
    turn = ((2 * a + 1) * u) & 255
    table = jnp.cos(turn.astype(f32) * f32(jnp.pi / 128)) * f32((2.0 / CH) ** 0.5)
    return jnp.where(u == 0, f32((1.0 / CH) ** 0.5), table)


def pick(table, row):
    n = row.shape[1]
    hot = (lax.broadcasted_iota(jnp.int32, (CH, n), 0) == jnp.broadcast_to(row, (CH, n))).astype(f32)
    return dot(table, hot, NN, lax.Precision.HIGHEST)


def rep_of(c, q, p):
    return (1 - c) * (q * 8 + p * 2) + c * (p * 8 + q * 2 + 1)


def first_kernel(
    x_hbm, g_hbm, w_hbm, mom_hbm, sel_ref,
    m_ref, grad_ref, eh_ref, el_ref, call_ref, wv,
    xv, gv, but, bvt, bve, bu4, cown,
    local_sem, g_send, g_recv, c_send, c_recv,
):
    feat = lax.axis_index("feat")
    rep = lax.axis_index("rep")
    c = rep % 2
    z = (rep // 2) % 4
    y = rep // 8
    p = (1 - c) * z + c * y
    q = (1 - c) * y + c * z
    slot = c * 16 + q * 4 + p
    right, left, across = (feat + 1) % 4, (feat + 3) % 4, (feat + 2) % 4
    near = [rep_of(c, q, (p + s) % 4) for s in (1, 2, 3)]
    far = [rep_of(c, (q + s) % 4, p) for s in (1, 2, 3)]
    partner = rep + 1 - 2 * c

    blocks = (feat, left, right, across)
    own_g = pltpu.make_async_copy(g_hbm, gv.at[pl.ds(feat * 256, 256)], local_sem.at[0])
    own_g.start()
    x_copies = []
    for n, b in enumerate(blocks):
        rows = pl.ds(b * 256, 256)
        x_copies.append(pltpu.make_async_copy(x_hbm.at[rows], xv.at[rows], local_sem.at[1 + n]))
    w_copies = [
        pltpu.make_async_copy(w_hbm.at[:, pl.ds(n * 128, 128)], wv.at[n], local_sem.at[7 + n]) for n in range(4)
    ]
    m_copy = pltpu.make_async_copy(mom_hbm, m_ref, local_sem.at[5])
    x_copies[0].start()
    for cp in w_copies:
        cp.start()
    m_copy.start()
    for cp in x_copies[1:]:
        cp.start()

    barrier = pltpu.get_barrier_semaphore()
    for f in (left, right):
        pl.semaphore_signal(barrier, inc=1, device_id={"feat": f})
    for r in near + far + [partner]:
        pl.semaphore_signal(barrier, inc=1, device_id={"rep": r})
    pl.semaphore_wait(barrier, 9)

    def g_copy(n, block, half, to, src=None):
        rows = pl.ds(block * 256 + half * 128, 128)
        return pltpu.make_async_remote_copy(
            src_ref=gv.at[rows] if src is None else src,
            dst_ref=gv.at[rows],
            send_sem=g_send.at[n],
            recv_sem=g_recv.at[n],
            device_id={"feat": to},
        )

    sends = [
        g_copy(0, feat, 0, right, g_hbm.at[pl.ds(0, 128)]),
        g_copy(1, feat, 1, left, g_hbm.at[pl.ds(128, 128)]),
        g_copy(2, feat, 1, right, g_hbm.at[pl.ds(128, 128)]),
        g_copy(3, feat, 0, left, g_hbm.at[pl.ds(0, 128)]),
    ]
    for cp in sends:
        cp.start()
    arrive = [
        g_copy(0, left, 0, right),
        g_copy(1, right, 1, left),
        g_copy(2, left, 1, right),
        g_copy(3, right, 0, left),
        g_copy(4, across, 0, right),
        g_copy(5, across, 1, left),
    ]

    table = dct_transposed()
    sel = sel_ref[...]
    rows = []
    for s in range(32):
        r = rep_of(s // 16, (s % 16) // 4, s % 4)
        rows.append(sel[r : r + 1, :])
    flat = jnp.concatenate(rows, axis=1)
    but[...] = pick(table, flat >> 6)
    bvt[...] = pick(table, flat & 63)
    mine = sel_ref[pl.ds(rep, 1), :]
    mine = jnp.concatenate([mine] * 4, axis=1)
    bu4[...] = pick(table, mine >> 6)
    bv4 = pick(table, mine & 63)
    tall = jnp.concatenate([bv4] * 4, axis=0)
    ahead = lax.broadcasted_iota(jnp.int32, (256, 128), 0) // 64
    along = lax.broadcasted_iota(jnp.int32, (256, 128), 1) // 32
    bve[...] = jnp.where(ahead == along, tall, f32(0))

    def outer(a):
        high, low = split(but[pl.ds(a, 1), :] * bvt[...])
        at = pl.ds(pl.multiple_of(a * CH, CH), CH)
        eh_ref[at, :] = high
        el_ref[at, :] = low

    @pl.loop(0, 24)
    def _(a):
        outer(a)

    arrive[0].wait_recv()
    forward_right = g_copy(4, left, 0, right)
    forward_right.start()
    arrive[1].wait_recv()
    forward_left = g_copy(5, right, 1, left)
    forward_left.start()

    @pl.loop(24, 64)
    def _(a):
        outer(a)

    def weight_grad(block, first):
        rows = pl.ds(pl.multiple_of(block * 256, 256), 256)

        @pl.loop(0, 8)
        def _(n):
            at = pl.ds(pl.multiple_of(n * 256, 256), 256)
            part = dot(xv[rows, at], gv[rows, :], TN) * f32(1.0 / 1024)
            if first:
                m_ref[at, :] = f32(MOMENTUM_DECAY) * m_ref[at, :] + part
            else:
                m_ref[at, :] = m_ref[at, :] + part

    def input_grad(block, n0, n1):
        rows = pl.ds(pl.multiple_of(block * 256, 256), 256)

        @pl.loop(n0, n1)
        def _(step):
            at = pl.ds(pl.multiple_of(step * 256, 256), 256)
            high, low = split(jnp.concatenate([wv[n, at, :] for n in range(4)], axis=1))
            gb = gv[rows, :]
            grad_ref[rows, at] = dot(gb, high, NT) + dot(gb, low, NT)

    own_g.wait()
    x_copies[0].wait()
    m_copy.wait()
    weight_grad(feat, True)
    for cp in w_copies:
        cp.wait()
    input_grad(feat, 0, 8)
    arrive[2].wait_recv()
    x_copies[1].wait()
    weight_grad(left, False)
    arrive[3].wait_recv()
    x_copies[2].wait()
    weight_grad(right, False)
    input_grad(left, 0, 8)
    input_grad(right, 0, 8)
    arrive[4].wait_recv()
    arrive[5].wait_recv()
    x_copies[3].wait()
    weight_grad(across, False)

    @pl.loop(0, 4)
    def _(n):
        at = pl.ds(pl.multiple_of(n * 512, 512), 512)
        to = pl.ds(pl.multiple_of(n * 8, 8), 8)
        for h in range(2):
            inner = dot(m_ref[at, h * 256 : h * 256 + 256], bve[...], NN, lax.Precision.HIGH)
            cown[to, h * 128 : h * 128 + 128] = jnp.sum(inner.reshape(8, CH, 128) * bu4[...][None], axis=1)

    turned = cown[...].T
    call_ref[slot] = jnp.concatenate([turned[j * 32 : j * 32 + 32, :] for j in range(8)], axis=1)

    def c_copy(n, at, to):
        return pltpu.make_async_remote_copy(
            src_ref=call_ref.at[at],
            dst_ref=call_ref.at[at],
            send_sem=c_send.at[n],
            recv_sem=c_recv.at[at],
            device_id={"rep": to},
        )

    out = []

    def send(at, to):
        cp = c_copy(len(out), at, to)
        cp.start()
        out.append(cp)

    for r in near + far + [partner]:
        send(slot, r)

    def take_away(n0, n1):
        @pl.loop(n0, n1)
        def _(n):
            at = pl.ds(pl.multiple_of(n * 512, 512), 512)
            to = pl.ds(pl.multiple_of(n * 8, 8), 8)
            for h in range(2):
                cols = slice(h * 256, h * 256 + 256)
                field = cown[to, h * 128 : h * 128 + 128][:, None, :] * bu4[...][None]
                back = dot(field.reshape(512, 128), bve[...], NT, lax.Precision.HIGH)
                m_ref[at, cols] = m_ref[at, cols] - back

    input_grad(across, 0, 4)
    for s in (1, 3, 2):
        at = c * 16 + q * 4 + (p + s) % 4
        c_copy(0, at, partner).wait_recv()
        for r in far + [partner]:
            send(at, r)
    input_grad(across, 4, 8)
    take_away(0, 4)
    for t in range(4):
        for s in (1, 3, 2):
            at = c * 16 + ((q + s) % 4) * 4 + (p + t) % 4
            c_copy(0, at, partner).wait_recv()
            send(at, partner)
    for n in range(16):
        c_copy(0, (1 - c) * 16 + n, partner).wait_recv()
    for cp in sends + [forward_right, forward_left] + out:
        cp.wait_send()


def second_kernel(
    m_ref, grad_ref, eh_ref, el_ref, call_ref, w_ref, grad_hbm, res_hbm, new_hbm, nw, lh, ll, sems
):
    copies = [
        pltpu.make_async_copy(m_ref, res_hbm, sems.at[0]),
        pltpu.make_async_copy(grad_ref, grad_hbm, sems.at[1]),
    ]
    for cp in copies:
        cp.start()
    high, low = split(call_ref[...].reshape(1024, 256).T)
    lh[...] = high
    ll[...] = low
    low_half = lax.broadcasted_iota(jnp.int32, (32, 128), 1) < 64

    @pl.loop(0, 16)
    def _(n):
        at = pl.ds(pl.multiple_of(n * 256, 256), 256)
        eh = eh_ref[at, :]
        total = dot(lh[...], eh, NT) + dot(ll[...], eh, NT) + dot(lh[...], el_ref[at, :], NT)
        total = total * f32(STEP_RATE)
        for h in range(2):
            for j in range(4):
                one = total[j * 64 : j * 64 + 32, h * 128 : h * 128 + 128]
                two = total[j * 64 + 32 : j * 64 + 64, h * 128 : h * 128 + 128]
                even = jnp.where(low_half, one, pltpu.roll(two, 64, 1))
                odd = jnp.where(low_half, pltpu.roll(one, 64, 1), two)
                for k, v in enumerate((even, odd)):
                    rows = pl.ds(n * 4 + h * 2 + k, 32, stride=CH)
                    nw[j, rows, :] = w_ref[j, rows, :] - v

    for n in range(4):
        cp = pltpu.make_async_copy(nw.at[n], new_hbm.at[:, pl.ds(n * 128, 128)], sems.at[2 + n])
        cp.start()
        copies.append(cp)
    for cp in copies:
        cp.wait()


def vmem(shape, dtype):
    return pltpu.VMEM(shape, dtype)


def body(x, g, w, mom, sel):
    any_space = pl.BlockSpec(memory_space=pl.ANY)
    vm = pl.BlockSpec(memory_space=pltpu.VMEM)
    mid = pl.pallas_call(
        first_kernel,
        out_shape=(
            vmem((2048, 512), f32),
            vmem((1024, 2048), f32),
            vmem((4096, 1024), bf16),
            vmem((4096, 1024), bf16),
            vmem((32, 32, 256), f32),
            vmem((4, 2048, 128), f32),
        ),
        in_specs=[any_space] * 4 + [vm],
        out_specs=[vm] * 6,
        scratch_shapes=[
            pltpu.VMEM((1024, 2048), bf16),
            pltpu.VMEM((1024, 512), bf16),
            pltpu.VMEM((CH, 1024), f32),
            pltpu.VMEM((CH, 1024), f32),
            pltpu.VMEM((256, 128), f32),
            pltpu.VMEM((CH, 128), f32),
            pltpu.VMEM((32, 256), f32),
            pltpu.SemaphoreType.DMA((11,)),
            pltpu.SemaphoreType.DMA((6,)),
            pltpu.SemaphoreType.DMA((6,)),
            pltpu.SemaphoreType.DMA((31,)),
            pltpu.SemaphoreType.DMA((32,)),
        ],
        compiler_params=pltpu.CompilerParams(
            collective_id=0, has_side_effects=True, vmem_limit_bytes=12 * MIB
        ),
        name="gather_and_select",
    )(*(pltpu.with_memory_space_constraint(v, pltpu.HBM) for v in (x, g, w, mom[0])), sel)
    grad, res, new = pl.pallas_call(
        second_kernel,
        out_shape=(
            jax.ShapeDtypeStruct((1024, 2048), f32),
            jax.ShapeDtypeStruct((2048, 512), f32),
            jax.ShapeDtypeStruct((2048, 512), f32),
        ),
        in_specs=[vm] * 6,
        out_specs=[any_space] * 3,
        scratch_shapes=[
            pltpu.VMEM((4, 2048, 128), f32),
            pltpu.VMEM((256, 1024), bf16),
            pltpu.VMEM((256, 1024), bf16),
            pltpu.SemaphoreType.DMA((6,)),
        ],
        compiler_params=pltpu.CompilerParams(vmem_limit_bytes=12 * MIB),
        name="decode_and_write",
    )(*(pltpu.with_memory_space_constraint(v, pltpu.VMEM) for v in mid))
    return grad, res[None], new


def solution(mesh):
    in_specs = (P("rep", "feat"), P(("rep", "feat"), None), P("feat", None), P("rep", "feat", None), P())
    out_specs = (P("rep", "feat"), P("rep", "feat", None), P("feat", None))
    return jax.shard_map(body, mesh=mesh, in_specs=in_specs, out_specs=out_specs, check_vma=False)
```

```python
import functools

import jax
import jax.numpy as jnp
from jax import lax
from jax.experimental import pallas as pl
from jax.experimental.pallas import tpu as pltpu
from jax.sharding import PartitionSpec as P

CH = 64
MOMENTUM_DECAY = 0.9
STEP_RATE = 0.5
f32 = jnp.float32
bf16 = jnp.bfloat16
NN = (((1,), (0,)), ((), ()))
NT = (((1,), (1,)), ((), ()))
TN = (((0,), (0,)), ((), ()))
MIB = 1 << 20


def dot(a, b, dims, precision=None):
    return lax.dot_general(a, b, dims, precision=precision, preferred_element_type=f32)


def split(v):
    high = v.astype(bf16)
    return high, (v - high.astype(f32)).astype(bf16)


def dct_transposed():
    a = lax.broadcasted_iota(jnp.int32, (CH, CH), 0)
    u = lax.broadcasted_iota(jnp.int32, (CH, CH), 1)
    turn = ((2 * a + 1) * u) & 255
    table = jnp.cos(turn.astype(f32) * f32(jnp.pi / 128)) * f32((2.0 / CH) ** 0.5)
    return jnp.where(u == 0, f32((1.0 / CH) ** 0.5), table)


def pick(table, row):
    n = row.shape[1]
    hot = (lax.broadcasted_iota(jnp.int32, (CH, n), 0) == jnp.broadcast_to(row, (CH, n))).astype(f32)
    return dot(table, hot, NN, lax.Precision.HIGHEST)


def offsets():
    both = [(dy, dz) for dy in range(4) for dz in range(4) if (dy, dz) != (0, 0)]
    return sorted(both, key=lambda o: (min(o[0], 4 - o[0]) + min(o[1], 4 - o[1]), o))


def first_kernel(
    x_hbm, g_hbm, w_hbm, mom_hbm, sel_ref,
    m_ref, grad_ref, eh_ref, el_ref, oth_ref, acc_ref, wv,
    xv, xt, gv, but, bvt, bhl, bhh, bu4, cown, own_ref,
    local_sem, g_send, g_recv, c_send, own_recv, oth_recv,
):
    feat = lax.axis_index("feat")
    rep = lax.axis_index("rep")
    core = rep % 2
    chip = rep // 2
    y, z = chip // 4, chip % 4
    partner = rep + 1 - 2 * core
    right, left, across = (feat + 1) % 4, (feat + 3) % 4, (feat + 2) % 4
    blocks = (feat, left, right, across)

    def chip_at(dy, dz):
        return (y + dy) % 4 * 4 + (z + dz) % 4

    own_g = pltpu.make_async_copy(g_hbm, gv.at[pl.ds(0, 256)], local_sem.at[0])
    own_g.start()
    x_copies = [
        pltpu.make_async_copy(x_hbm.at[pl.ds(b * 256, 256)], xv.at[pl.ds(n * 256, 256)], local_sem.at[1 + n])
        for n, b in enumerate(blocks)
    ]
    m_copy = pltpu.make_async_copy(mom_hbm, m_ref, local_sem.at[5])
    w_copies = [
        pltpu.make_async_copy(w_hbm.at[:, pl.ds(n * 128, 128)], wv.at[n], local_sem.at[6 + n]) for n in range(4)
    ]
    for cp in x_copies + w_copies + [m_copy]:
        cp.start()

    barrier = pltpu.get_barrier_semaphore()
    for f in (left, right):
        pl.semaphore_signal(barrier, inc=1, device_id={"feat": f})
    for dy, dz in offsets():
        pl.semaphore_signal(barrier, inc=1, device_id={"rep": chip_at(dy, dz) * 2 + core})
    pl.semaphore_signal(barrier, inc=1, device_id={"rep": partner})

    table = dct_transposed()
    rows = []
    for s in range(32):
        plane = core if s < 16 else 1 - core
        rows.append(sel_ref[pl.ds((s % 16) * 2 + plane, 1), :])
    flat = jnp.concatenate(rows, axis=1)
    but[...] = pick(table, flat >> 6)
    bvt[...] = pick(table, flat & 63)
    mine = sel_ref[pl.ds(rep, 1), :]
    mine = jnp.concatenate([mine] * 4, axis=1)
    bu4[...] = pick(table, mine >> 6)
    tall = jnp.concatenate([pick(table, mine & 63)] * 4, axis=0)
    ahead = lax.broadcasted_iota(jnp.int32, (256, 128), 0) // 64
    along = lax.broadcasted_iota(jnp.int32, (256, 128), 1) // 32
    high, low = split(jnp.where(ahead == along, tall, f32(0)))
    bhl[:, :128] = high
    bhl[:, 128:] = low
    bhh[:, :128] = high
    bhh[:, 128:] = high

    pl.semaphore_wait(barrier, 18)

    def g_copy(n, slot, half, to, src=None):
        rows = pl.ds(slot * 256 + half * 128, 128)
        return pltpu.make_async_remote_copy(
            src_ref=src,
            dst_ref=gv.at[rows],
            send_sem=g_send.at[n],
            recv_sem=g_recv.at[n],
            device_id={"feat": to},
        )

    halves = [g_hbm.at[pl.ds(0, 128)], g_hbm.at[pl.ds(128, 128)]]
    sends = [
        g_copy(0, 1, 0, right, halves[0]),
        g_copy(1, 2, 1, left, halves[1]),
        g_copy(2, 1, 1, right, halves[1]),
        g_copy(3, 2, 0, left, halves[0]),
    ]
    for cp in sends:
        cp.start()
    sends.append(g_copy(4, 3, 0, right, gv.at[pl.ds(256, 128)]))
    sends.append(g_copy(5, 3, 1, left, gv.at[pl.ds(512 + 128, 128)]))

    def outer(a):
        high, low = split(but[pl.ds(a, 1), :] * bvt[...])
        at = pl.ds(pl.multiple_of(a * CH, CH), CH)
        eh_ref[at, :] = high
        el_ref[at, :] = low

    def turn(slot):
        x_copies[slot].wait()

        @pl.loop(0, 8)
        def _(n):
            at = pl.ds(pl.multiple_of(n * 256, 256), 256)
            xt[slot, at, :] = xv[slot * 256 : slot * 256 + 256, at].T

    turn(0)

    @pl.loop(0, 36)
    def _(a):
        outer(a)

    sends[0].wait_recv()
    sends[4].start()
    sends[1].wait_recv()
    sends[5].start()

    @pl.loop(36, 64)
    def _(a):
        outer(a)

    for slot in (1, 2, 3):
        turn(slot)
    own_g.wait()
    m_copy.wait()
    sends[2].wait_recv()
    sends[3].wait_recv()
    for n in range(4):
        at = slice(n * 512, n * 512 + 512)
        lhs = jnp.concatenate([xt[s, at, :] for s in range(3)], axis=1)
        m_ref[at, :] = f32(MOMENTUM_DECAY) * m_ref[at, :] + dot(lhs, gv[0:768, :], NN) * f32(1.0 / 1024)
    sends[4].wait_recv()
    sends[5].wait_recv()
    for n in range(4):
        at = slice(n * 512, n * 512 + 512)
        m_ref[at, :] = m_ref[at, :] + dot(xt[3, at, :], gv[768:1024, :], NN) * f32(1.0 / 1024)

    for n in range(4):
        for h in range(2):
            high, low = split(m_ref[n * 512 : n * 512 + 512, h * 256 : h * 256 + 256])
            wide = dot(high, bhl[...], NN)
            inner = wide[:, :128] + wide[:, 128:] + dot(low, bhl[:, :128], NN)
            cown[n * 8 : n * 8 + 8, h * 128 : h * 128 + 128] = jnp.sum(
                inner.reshape(8, CH, 128) * bu4[...][None], axis=1
            )
    turned = cown[...].T
    own_ref[chip] = jnp.concatenate([turned[j * 32 : j * 32 + 32, :] for j in range(8)], axis=1)

    gone = []

    def send(dst, sem, at, to):
        cp = pltpu.make_async_remote_copy(
            src_ref=own_ref.at[at],
            dst_ref=dst.at[at],
            send_sem=c_send.at[len(gone)],
            recv_sem=sem.at[at],
            device_id={"rep": to},
        )
        cp.start()
        gone.append(cp)

    def arrived(ref, sem, at):
        pltpu.make_async_remote_copy(
            src_ref=ref.at[at], dst_ref=ref.at[at], send_sem=c_send.at[0], recv_sem=sem.at[at],
            device_id={"rep": partner},
        ).wait_recv()

    for dy, dz in offsets():
        send(own_ref, own_recv, chip, chip_at(dy, dz) * 2 + core)
    send(oth_ref, oth_recv, chip, partner)

    def pass_on(n0, n1):
        for dy, dz in offsets()[n0:n1]:
            at = chip_at(-dy, -dz)
            arrived(own_ref, own_recv, at)
            send(oth_ref, oth_recv, at, partner)

    def take_away(n):
        for h in range(2):
            at, cols = slice(n * 512, n * 512 + 512), slice(h * 256, h * 256 + 256)
            field = cown[n * 8 : n * 8 + 8, h * 128 : h * 128 + 128][:, None, :] * bu4[...][None]
            high, low = split(field.reshape(512, 128))
            back = dot(jnp.concatenate([high, low], axis=1), bhh[...], NT) + dot(high, bhl[:, 128:], NT)
            m_ref[at, cols] = m_ref[at, cols] - back

    def input_grad(n):
        cols = slice(n * 512, n * 512 + 512)
        high, low = split(jnp.concatenate([wv[k, cols, :] for k in range(4)], axis=1))
        part = dot(gv[...], high, NT) + dot(gv[...], low, NT)
        for s, b in enumerate(blocks):
            grad_ref[pl.ds(pl.multiple_of(b * 256, 256), 256), cols] = part[s * 256 : s * 256 + 256, :]

    for n in range(4):
        take_away(n)
    for cp in w_copies:
        cp.wait()
    input_grad(0)
    pass_on(0, 4)
    input_grad(1)
    pass_on(4, 8)
    input_grad(2)
    pass_on(8, 12)
    input_grad(3)
    pass_on(12, 15)

    high, low = split(own_ref[...].reshape(512, 256).T)
    for n in range(8):
        at = slice(n * 512, n * 512 + 512)
        eh = eh_ref[at, 0:512]
        acc_ref[:, at] = dot(high, eh, NT) + dot(low, eh, NT) + dot(high, el_ref[at, 0:512], NT)

    for n in range(16):
        arrived(oth_ref, oth_recv, n)
    for cp in sends + gone:
        cp.wait_send()


def second_kernel(
    m_ref, grad_ref, eh_ref, el_ref, oth_ref, acc_ref, w_ref, grad_hbm, res_hbm, new_hbm, nw, sems
):
    copies = [
        pltpu.make_async_copy(m_ref, res_hbm, sems.at[0]),
        pltpu.make_async_copy(grad_ref, grad_hbm, sems.at[1]),
    ]
    for cp in copies:
        cp.start()
    high, low = split(oth_ref[...].reshape(512, 256).T)
    low_half = lax.broadcasted_iota(jnp.int32, (32, 128), 1) < 64
    for n in range(8):
        at = slice(n * 512, n * 512 + 512)
        eh = eh_ref[at, 512:]
        total = acc_ref[:, at] + dot(high, eh, NT) + dot(low, eh, NT) + dot(high, el_ref[at, 512:], NT)
        total = total * f32(STEP_RATE)
        for h in range(4):
            for j in range(4):
                one = total[j * 64 : j * 64 + 32, h * 128 : h * 128 + 128]
                two = total[j * 64 + 32 : j * 64 + 64, h * 128 : h * 128 + 128]
                even = jnp.where(low_half, one, pltpu.roll(two, 64, 1))
                odd = jnp.where(low_half, pltpu.roll(one, 64, 1), two)
                for k, v in enumerate((even, odd)):
                    rows = pl.ds(n * 8 + h * 2 + k, 32, stride=CH)
                    nw[j, rows, :] = w_ref[j, rows, :] - v
    for n in range(4):
        cp = pltpu.make_async_copy(nw.at[n], new_hbm.at[:, pl.ds(n * 128, 128)], sems.at[2 + n])
        cp.start()
        copies.append(cp)
    for cp in copies:
        cp.wait()


def vmem(shape, dtype):
    return pltpu.VMEM(shape, dtype)


def body(x, g, w, mom, sel):
    any_space = pl.BlockSpec(memory_space=pl.ANY)
    vm = pl.BlockSpec(memory_space=pltpu.VMEM)
    mid = pl.pallas_call(
        first_kernel,
        out_shape=(
            vmem((2048, 512), f32),
            vmem((1024, 2048), f32),
            vmem((4096, 1024), bf16),
            vmem((4096, 1024), bf16),
            vmem((16, 32, 256), f32),
            vmem((256, 4096), f32),
            vmem((4, 2048, 128), f32),
        ),
        in_specs=[any_space] * 4 + [vm],
        out_specs=[vm] * 7,
        scratch_shapes=[
            pltpu.VMEM((1024, 2048), bf16),
            pltpu.VMEM((4, 2048, 256), bf16),
            pltpu.VMEM((1024, 512), bf16),
            pltpu.VMEM((CH, 1024), f32),
            pltpu.VMEM((CH, 1024), f32),
            pltpu.VMEM((256, 256), bf16),
            pltpu.VMEM((256, 256), bf16),
            pltpu.VMEM((CH, 128), f32),
            pltpu.VMEM((32, 256), f32),
            pltpu.VMEM((16, 32, 256), f32),
            pltpu.SemaphoreType.DMA((10,)),
            pltpu.SemaphoreType.DMA((6,)),
            pltpu.SemaphoreType.DMA((6,)),
            pltpu.SemaphoreType.DMA((31,)),
            pltpu.SemaphoreType.DMA((16,)),
            pltpu.SemaphoreType.DMA((16,)),
        ],
        compiler_params=pltpu.CompilerParams(
            collective_id=0, has_side_effects=True, vmem_limit_bytes=15 * MIB
        ),
        name="gather_and_select",
    )(*(pltpu.with_memory_space_constraint(v, pltpu.HBM) for v in (x, g, w, mom[0])), sel)
    grad, res, new = pl.pallas_call(
        second_kernel,
        out_shape=(
            jax.ShapeDtypeStruct((1024, 2048), f32),
            jax.ShapeDtypeStruct((2048, 512), f32),
            jax.ShapeDtypeStruct((2048, 512), f32),
        ),
        in_specs=[vm] * 7,
        out_specs=[any_space] * 3,
        scratch_shapes=[
            pltpu.VMEM((4, 2048, 128), f32),
            pltpu.SemaphoreType.DMA((6,)),
        ],
        compiler_params=pltpu.CompilerParams(vmem_limit_bytes=12 * MIB),
        name="decode_and_write",
    )(*(pltpu.with_memory_space_constraint(v, pltpu.VMEM) for v in mid))
    return grad, res[None], new


def solution(mesh):
    in_specs = (P("rep", "feat"), P(("rep", "feat"), None), P("feat", None), P("rep", "feat", None), P())
    out_specs = (P("rep", "feat"), P("rep", "feat", None), P("feat", None))
    return jax.shard_map(body, mesh=mesh, in_specs=in_specs, out_specs=out_specs, check_vma=False)
```

```python
import functools

import jax
import jax.numpy as jnp
from jax import lax
from jax.experimental import pallas as pl
from jax.experimental.pallas import tpu as pltpu
from jax.sharding import PartitionSpec as P

CH = 64
MOMENTUM_DECAY = 0.9
STEP_RATE = 0.5
f32 = jnp.float32
bf16 = jnp.bfloat16
NN = (((1,), (0,)), ((), ()))
NT = (((1,), (1,)), ((), ()))
TN = (((0,), (0,)), ((), ()))
MIB = 1 << 20


def dot(a, b, dims, precision=None):
    return lax.dot_general(a, b, dims, precision=precision, preferred_element_type=f32)


def split(v):
    high = v.astype(bf16)
    return high, (v - high.astype(f32)).astype(bf16)


def dct_transposed():
    a = lax.broadcasted_iota(jnp.int32, (CH, CH), 0)
    u = lax.broadcasted_iota(jnp.int32, (CH, CH), 1)
    turn = ((2 * a + 1) * u) & 255
    table = jnp.cos(turn.astype(f32) * f32(jnp.pi / 128)) * f32((2.0 / CH) ** 0.5)
    return jnp.where(u == 0, f32((1.0 / CH) ** 0.5), table)


def pick(table, row):
    n = row.shape[1]
    hot = (lax.broadcasted_iota(jnp.int32, (CH, n), 0) == jnp.broadcast_to(row, (CH, n))).astype(f32)
    return dot(table, hot, NN, lax.Precision.HIGHEST)


def offsets():
    both = [(dy, dz) for dy in range(4) for dz in range(4) if (dy, dz) != (0, 0)]
    return sorted(both, key=lambda o: (min(o[0], 4 - o[0]) + min(o[1], 4 - o[1]), o))


def first_kernel(
    x_hbm, g_hbm, w_hbm, mom_hbm, sel_hbm,
    m_ref, grad_ref, eh_ref, el_ref, sign_ref, own_ref, oth_ref, nw, wv, gv,
    xv, xt, sel_ref, but, bvt, bhl, bhh, bu4, cown, lh, ll,
    local_sem, g_send, g_recv, c_send, own_recv, oth_recv,
):
    feat = lax.axis_index("feat")
    rep = lax.axis_index("rep")
    core = rep % 2
    chip = rep // 2
    y, z = chip // 4, chip % 4
    partner = rep + 1 - 2 * core
    right, left, across = (feat + 1) % 4, (feat + 3) % 4, (feat + 2) % 4
    blocks = (feat, left, right, across)

    def chip_at(dy, dz):
        return (y + dy) % 4 * 4 + (z + dz) % 4

    barrier = pltpu.get_barrier_semaphore()
    for f in (left, right):
        pl.semaphore_signal(barrier, inc=1, device_id={"feat": f})
    for dy, dz in offsets():
        pl.semaphore_signal(barrier, inc=1, device_id={"rep": chip_at(dy, dz) * 2 + core})
    pl.semaphore_signal(barrier, inc=1, device_id={"rep": partner})

    sel_copy = pltpu.make_async_copy(sel_hbm, sel_ref, local_sem.at[0])
    own_g = [
        pltpu.make_async_copy(g_hbm.at[:, pl.ds(h * 256, 256)], gv.at[h, pl.ds(0, 256)], local_sem.at[1 + h])
        for h in range(2)
    ]
    x_copies = [
        pltpu.make_async_copy(x_hbm.at[pl.ds(b * 256, 256)], xv.at[pl.ds(n * 256, 256)], local_sem.at[3 + n])
        for n, b in enumerate(blocks)
    ]
    m_copy = pltpu.make_async_copy(mom_hbm, m_ref, local_sem.at[7])
    w_copies = [
        pltpu.make_async_copy(w_hbm.at[:, pl.ds(n * 128, 128)], wv.at[n], local_sem.at[8 + n]) for n in range(4)
    ]
    for cp in [sel_copy] + x_copies + own_g + [m_copy] + w_copies:
        cp.start()

    def g_copy(h, n, slot, half, to, forward=None):
        if forward is None:
            src = g_hbm.at[pl.ds(half * 128, 128), pl.ds(h * 256, 256)]
        else:
            src = gv.at[h, pl.ds(forward * 256 + half * 128, 128)]
        return pltpu.make_async_remote_copy(
            src_ref=src,
            dst_ref=gv.at[h, pl.ds(slot * 256 + half * 128, 128)],
            send_sem=g_send.at[h * 6 + n],
            recv_sem=g_recv.at[h * 6 + n],
            device_id={"feat": to},
        )

    sends = [
        [
            g_copy(h, 0, 1, 0, right),
            g_copy(h, 1, 2, 1, left),
            g_copy(h, 2, 1, 1, right),
            g_copy(h, 3, 2, 0, left),
            g_copy(h, 4, 3, 0, right, 1),
            g_copy(h, 5, 3, 1, left, 2),
        ]
        for h in range(2)
    ]
    pl.semaphore_wait(barrier, 18)
    for cp in sends[0][:4] + sends[1][:2]:
        cp.start()

    def forward(h):
        for n in range(2):
            sends[h][n].wait_recv()
            sends[h][4 + n].start()

    table = dct_transposed()
    sel_copy.wait()
    rows = []
    for s in range(32):
        plane = core if s < 16 else 1 - core
        rows.append(sel_ref[pl.ds((s % 16) * 2 + plane, 1), :])
    flat = jnp.concatenate(rows, axis=1)
    but[...] = pick(table, flat >> 6)
    bvt[...] = pick(table, flat & 63)
    sign_ref[...] = jnp.broadcast_to(f32(1) - f32(2) * ((flat >> 6) & 1).astype(f32), (8, 1024))
    mine = sel_ref[pl.ds(rep, 1), :]
    mine = jnp.concatenate([mine] * 4, axis=1)
    bu4[...] = pick(table, mine >> 6)
    tall = jnp.concatenate([pick(table, mine & 63)] * 4, axis=0)
    ahead = lax.broadcasted_iota(jnp.int32, (256, 128), 0) // 64
    along = lax.broadcasted_iota(jnp.int32, (256, 128), 1) // 32
    high, low = split(jnp.where(ahead == along, tall, f32(0)))
    bhl[:, :128] = high
    bhl[:, 128:] = low
    bhh[:, :128] = high
    bhh[:, 128:] = high

    for slot in range(4):
        x_copies[slot].wait()

        @pl.loop(0, 8)
        def _(n):
            a = slot * 8 + n
            high, low = split(but[pl.ds(a, 1), :] * bvt[...])
            to = pl.ds(pl.multiple_of(a * CH, CH), CH)
            eh_ref[to, :] = high
            el_ref[to, :] = low
            at = pl.ds(pl.multiple_of(n * 256, 256), 256)
            xt[slot, at, :] = xv[slot * 256 : slot * 256 + 256, at].T

        if slot == 2:
            forward(0)
            for cp in sends[1][2:4]:
                cp.start()

    gone = []

    def send(h, dst, sem, at, to):
        cp = pltpu.make_async_remote_copy(
            src_ref=own_ref.at[h, at],
            dst_ref=dst.at[h, at],
            send_sem=c_send.at[len(gone)],
            recv_sem=sem.at[h * 16 + at],
            device_id={"rep": to},
        )
        cp.start()
        gone.append(cp)

    def arrived(h, ref, sem, at):
        pltpu.make_async_remote_copy(
            src_ref=ref.at[h, at], dst_ref=ref.at[h, at], send_sem=c_send.at[0], recv_sem=sem.at[h * 16 + at],
            device_id={"rep": partner},
        ).wait_recv()

    def pass_on(h, n0, n1):
        for dy, dz in offsets()[n0:n1]:
            at = chip_at(-dy, -dz)
            arrived(h, own_ref, own_recv, at)
            send(h, oth_ref, oth_recv, at, partner)

    def momentum(h):
        own_g[h].wait()
        sends[h][2].wait_recv()
        sends[h][3].wait_recv()
        if h == 0:
            m_copy.wait()
        cols = slice(h * 256, h * 256 + 256)
        for n in range(4):
            at = slice(n * 512, n * 512 + 512)
            lhs = jnp.concatenate([xt[s, at, :] for s in range(3)], axis=1)
            part = dot(lhs, gv[h, 0:768, :], NN) * f32(1.0 / 1024)
            m_ref[at, cols] = f32(MOMENTUM_DECAY) * m_ref[at, cols] + part

    def coefficients(h):
        sends[h][4].wait_recv()
        sends[h][5].wait_recv()
        cols = slice(h * 256, h * 256 + 256)
        for n in range(4):
            at = slice(n * 512, n * 512 + 512)
            value = m_ref[at, cols] + dot(xt[3, at, :], gv[h, 768:1024, :], NN) * f32(1.0 / 1024)
            m_ref[at, cols] = value
            high, low = split(value)
            wide = dot(high, bhl[...], NN)
            inner = wide[:, :128] + wide[:, 128:] + dot(low, bhl[:, :128], NN)
            cown[h, n * 8 : n * 8 + 8, :] = jnp.sum(inner.reshape(8, CH, 128) * bu4[...][None], axis=1)
        turned = cown[h].T
        own_ref[h, chip] = jnp.concatenate([turned[j * 32 : j * 32 + 32, :] for j in range(4)], axis=1)
        for dy, dz in offsets():
            send(h, own_ref, own_recv, chip, chip_at(dy, dz) * 2 + core)
        send(h, oth_ref, oth_recv, chip, partner)

    momentum(0)
    forward(1)
    coefficients(0)
    momentum(1)
    coefficients(1)

    def take_away(h):
        for n in range(4):
            at, cols = slice(n * 512, n * 512 + 512), slice(h * 256, h * 256 + 256)
            field = cown[h, n * 8 : n * 8 + 8, :][:, None, :] * bu4[...][None]
            high, low = split(field.reshape(512, 128))
            back = dot(jnp.concatenate([high, low], axis=1), bhh[...], NT) + dot(high, bhl[:, 128:], NT)
            m_ref[at, cols] = m_ref[at, cols] - back

    for cp in w_copies:
        cp.wait()
    take_away(0)
    pass_on(0, 0, 8)
    rows = [pl.ds(pl.multiple_of(b * 256, 256), 256) for b in blocks]
    input_grad(0, wv, gv, grad_ref, rows, 0)
    pass_on(0, 8, 15)
    take_away(1)
    pass_on(1, 0, 8)
    input_grad(1, wv, gv, grad_ref, rows, 1)
    pass_on(1, 8, 15)
    for n in range(16):
        arrived(0, oth_ref, oth_recv, n)
    fill(0, own_ref, oth_ref, sign_ref, lh, ll)
    for n in range(4):
        decode(0, n, eh_ref, el_ref, lh, ll, wv, nw)
    for n in range(16):
        arrived(1, oth_ref, oth_recv, n)
    for cp in sends[0] + sends[1] + gone:
        cp.wait_send()


def input_grad(n, wv, gv, to, rows, place):
    at = slice(n * 512, n * 512 + 512)
    part = None
    for h in range(2):
        high, low = split(jnp.concatenate([wv[2 * h, at, :], wv[2 * h + 1, at, :]], axis=1))
        new = dot(gv[h], high, NT) + dot(gv[h], low, NT)
        part = new if part is None else part + new
    for s in range(4):
        to[rows[s], place * 512 : place * 512 + 512] = part[s * 256 : s * 256 + 256, :]


def fill(h, own_ref, oth_ref, sign_ref, lh, ll):
    both = jnp.concatenate([own_ref[h].reshape(512, 128), oth_ref[h].reshape(512, 128)], axis=0)
    turned = both.T * f32(STEP_RATE)
    mirrored = turned * sign_ref[0:1, :]
    high, low = split(jnp.concatenate([turned, mirrored], axis=0))
    lh[...] = high
    ll[...] = low


def decode(h, n, eh_ref, el_ref, lh, ll, w_ref, nw):
    low_half = lax.broadcasted_iota(jnp.int32, (32, 128), 1) < 64
    at = slice(n * 512, n * 512 + 512)
    eh = eh_ref[at, :]
    total = dot(lh[...], eh, NT) + dot(ll[...], eh, NT) + dot(lh[...], el_ref[at, :], NT)
    for side in range(2):
        for k in range(4):
            for j in range(2):
                top = side * 128 + j * 64
                one = total[top : top + 32, k * 128 : k * 128 + 128]
                two = total[top + 32 : top + 64, k * 128 : k * 128 + 128]
                even = jnp.where(low_half, one, pltpu.roll(two, 64, 1))
                odd = jnp.where(low_half, pltpu.roll(one, 64, 1), two)
                for o, v in enumerate((even, odd)):
                    a = n * 8 + k * 2 + o
                    rows = pl.ds(63 - a if side else a, 32, stride=CH)
                    nw[j, rows, :] = w_ref[2 * h + j, rows, :] - v


def second_kernel(
    m_ref, grad_ref, eh_ref, el_ref, sign_ref, own_ref, oth_ref, new_ref, w_ref, gv,
    grad_hbm, res_hbm, new_hbm, rest, nw, lh, ll, sems,
):
    feat = lax.axis_index("feat")
    blocks = (feat, (feat + 3) % 4, (feat + 1) % 4, (feat + 2) % 4)
    rows = [pl.ds(pl.multiple_of(b * 256, 256), 256) for b in blocks]
    copies = []

    def start(src, dst):
        cp = pltpu.make_async_copy(src, dst, sems.at[len(copies)])
        cp.start()
        copies.append(cp)

    start(grad_ref, grad_hbm.at[:, pl.ds(0, 1024)])
    start(m_ref, res_hbm)
    for j in range(2):
        start(new_ref.at[j], new_hbm.at[:, pl.ds(j * 128, 128)])
    for n in range(2):
        input_grad(2 + n, w_ref, gv, rest, rows, n)
        start(rest.at[:, pl.ds(n * 512, 512)], grad_hbm.at[:, pl.ds(1024 + n * 512, 512)])
    fill(1, own_ref, oth_ref, sign_ref, lh, ll)
    for n in range(4):
        decode(1, n, eh_ref, el_ref, lh, ll, w_ref, nw)
    for j in range(2):
        start(nw.at[j], new_hbm.at[:, pl.ds(256 + j * 128, 128)])
    for cp in copies:
        cp.wait()


def vmem(shape, dtype):
    return pltpu.VMEM(shape, dtype)


def body(x, g, w, mom, sel):
    any_space = pl.BlockSpec(memory_space=pl.ANY)
    vm = pl.BlockSpec(memory_space=pltpu.VMEM)
    mid = pl.pallas_call(
        first_kernel,
        out_shape=(
            vmem((2048, 512), f32),
            vmem((1024, 1024), f32),
            vmem((2048, 1024), bf16),
            vmem((2048, 1024), bf16),
            vmem((8, 1024), f32),
            vmem((2, 16, 32, 128), f32),
            vmem((2, 16, 32, 128), f32),
            vmem((2, 2048, 128), f32),
            vmem((4, 2048, 128), f32),
            vmem((2, 1024, 256), bf16),
        ),
        in_specs=[any_space] * 5,
        out_specs=[vm] * 10,
        scratch_shapes=[
            pltpu.VMEM((1024, 2048), bf16),
            pltpu.VMEM((4, 2048, 256), bf16),
            pltpu.VMEM((32, 32), jnp.int32),
            pltpu.VMEM((CH, 1024), f32),
            pltpu.VMEM((CH, 1024), f32),
            pltpu.VMEM((256, 256), bf16),
            pltpu.VMEM((256, 256), bf16),
            pltpu.VMEM((CH, 128), f32),
            pltpu.VMEM((2, 32, 128), f32),
            pltpu.VMEM((256, 1024), bf16),
            pltpu.VMEM((256, 1024), bf16),
            pltpu.SemaphoreType.DMA((12,)),
            pltpu.SemaphoreType.DMA((12,)),
            pltpu.SemaphoreType.DMA((12,)),
            pltpu.SemaphoreType.DMA((62,)),
            pltpu.SemaphoreType.DMA((32,)),
            pltpu.SemaphoreType.DMA((32,)),
        ],
        compiler_params=pltpu.CompilerParams(
            collective_id=0, has_side_effects=True, vmem_limit_bytes=18 * MIB
        ),
        name="gather_and_select",
    )(*(pltpu.with_memory_space_constraint(v, pltpu.HBM) for v in (x, g, w, mom[0], sel)))
    grad, res, new = pl.pallas_call(
        second_kernel,
        out_shape=(
            jax.ShapeDtypeStruct((1024, 2048), f32),
            jax.ShapeDtypeStruct((2048, 512), f32),
            jax.ShapeDtypeStruct((2048, 512), f32),
        ),
        in_specs=[vm] * 10,
        out_specs=[any_space] * 3,
        scratch_shapes=[
            pltpu.VMEM((1024, 1024), f32),
            pltpu.VMEM((2, 2048, 128), f32),
            pltpu.VMEM((256, 1024), bf16),
            pltpu.VMEM((256, 1024), bf16),
            pltpu.SemaphoreType.DMA((16,)),
        ],
        compiler_params=pltpu.CompilerParams(vmem_limit_bytes=14 * MIB),
        name="decode_and_write",
    )(*(pltpu.with_memory_space_constraint(v, pltpu.VMEM) for v in mid))
    return grad, res[None], new


def solution(mesh):
    in_specs = (P("rep", "feat"), P(("rep", "feat"), None), P("feat", None), P("rep", "feat", None), P())
    out_specs = (P("rep", "feat"), P("rep", "feat", None), P("feat", None))
    return jax.shard_map(body, mesh=mesh, in_specs=in_specs, out_specs=out_specs, check_vma=False)
```

```python
import functools

import jax
import jax.numpy as jnp
from jax import lax
from jax.experimental import pallas as pl
from jax.experimental.pallas import tpu as pltpu
from jax.sharding import PartitionSpec as P

CH = 64
MOMENTUM_DECAY = 0.9
STEP_RATE = 0.5
f32 = jnp.float32
bf16 = jnp.bfloat16
NN = (((1,), (0,)), ((), ()))
NT = (((1,), (1,)), ((), ()))
TN = (((0,), (0,)), ((), ()))
MIB = 1 << 20


def dot(a, b, dims, precision=None):
    return lax.dot_general(a, b, dims, precision=precision, preferred_element_type=f32)


def split(v):
    high = v.astype(bf16)
    return high, (v - high.astype(f32)).astype(bf16)


def dct_transposed():
    a = lax.broadcasted_iota(jnp.int32, (CH, CH), 0)
    u = lax.broadcasted_iota(jnp.int32, (CH, CH), 1)
    turn = ((2 * a + 1) * u) & 255
    table = jnp.cos(turn.astype(f32) * f32(jnp.pi / 128)) * f32((2.0 / CH) ** 0.5)
    return jnp.where(u == 0, f32((1.0 / CH) ** 0.5), table)


def pick(table, row):
    n = row.shape[1]
    hot = (lax.broadcasted_iota(jnp.int32, (CH, n), 0) == jnp.broadcast_to(row, (CH, n))).astype(f32)
    return dot(table, hot, NN, lax.Precision.HIGHEST)


def offsets():
    both = [(dy, dz) for dy in range(4) for dz in range(4) if (dy, dz) != (0, 0)]
    return sorted(both, key=lambda o: (min(o[0], 4 - o[0]) + min(o[1], 4 - o[1]), o))


def first_kernel(
    x_hbm, g_hbm, w_hbm, mom_hbm, sel_hbm,
    m_ref, grad_ref, eh_ref, el_ref, sign_ref, own_ref, oth_ref, nw, wv, gv,
    xv, xt, sel_ref, but, bvt, bhl, bhh, bu4, cown, lh, ll,
    local_sem, g_send, g_recv, c_send, own_recv, oth_recv,
):
    feat = lax.axis_index("feat")
    rep = lax.axis_index("rep")
    core = rep % 2
    chip = rep // 2
    y, z = chip // 4, chip % 4
    partner = rep + 1 - 2 * core
    right, left, across = (feat + 1) % 4, (feat + 3) % 4, (feat + 2) % 4
    blocks = (feat, left, right, across)

    def chip_at(dy, dz):
        return (y + dy) % 4 * 4 + (z + dz) % 4

    barrier = pltpu.get_barrier_semaphore()
    for f in (left, right):
        pl.semaphore_signal(barrier, inc=1, device_id={"feat": f})
    for dy, dz in offsets():
        pl.semaphore_signal(barrier, inc=1, device_id={"rep": chip_at(dy, dz) * 2 + core})
    pl.semaphore_signal(barrier, inc=1, device_id={"rep": partner})

    sel_copy = pltpu.make_async_copy(sel_hbm, sel_ref, local_sem.at[0])
    own_g = [
        pltpu.make_async_copy(g_hbm.at[:, pl.ds(h * 256, 256)], gv.at[h, pl.ds(0, 256)], local_sem.at[1 + h])
        for h in range(2)
    ]
    x_copies = [
        pltpu.make_async_copy(x_hbm.at[pl.ds(b * 256, 256)], xv.at[pl.ds(n * 256, 256)], local_sem.at[3 + n])
        for n, b in enumerate(blocks)
    ]
    m_copy = pltpu.make_async_copy(mom_hbm, m_ref, local_sem.at[7])
    w_copies = [
        pltpu.make_async_copy(w_hbm.at[:, :, pl.ds(n * 128, 128)], wv.at[n], local_sem.at[8 + n]) for n in range(4)
    ]
    for cp in [sel_copy] + x_copies:
        cp.start()

    def g_copy(h, n, slot, half, to, forward=None):
        if forward is None:
            src = g_hbm.at[pl.ds(half * 128, 128), pl.ds(h * 256, 256)]
        else:
            src = gv.at[h, pl.ds(forward * 256 + half * 128, 128)]
        return pltpu.make_async_remote_copy(
            src_ref=src,
            dst_ref=gv.at[h, pl.ds(slot * 256 + half * 128, 128)],
            send_sem=g_send.at[h * 6 + n],
            recv_sem=g_recv.at[h * 6 + n],
            device_id={"feat": to},
        )

    sends = [
        [
            g_copy(h, 0, 1, 0, right),
            g_copy(h, 1, 2, 1, left),
            g_copy(h, 2, 1, 1, right),
            g_copy(h, 3, 2, 0, left),
            g_copy(h, 4, 3, 0, right, 1),
            g_copy(h, 5, 3, 1, left, 2),
        ]
        for h in range(2)
    ]
    pl.semaphore_wait(barrier, 18)
    for cp in sends[0][:4] + sends[1][:2]:
        cp.start()

    def forward(h):
        for n in range(2):
            sends[h][n].wait_recv()
            sends[h][4 + n].start()

    table = dct_transposed()
    sel_copy.wait()
    for cp in own_g + [m_copy]:
        cp.start()
    rows = []
    for s in range(32):
        plane = core if s < 16 else 1 - core
        rows.append(sel_ref[pl.ds((s % 16) * 2 + plane, 1), :])
    flat = jnp.concatenate(rows, axis=1)
    but[...] = pick(table, flat >> 6)
    bvt[...] = pick(table, flat & 63)
    sign_ref[...] = jnp.broadcast_to(f32(1) - f32(2) * ((flat >> 6) & 1).astype(f32), (8, 1024))
    mine = sel_ref[pl.ds(rep, 1), :]
    mine = jnp.concatenate([mine] * 4, axis=1)
    bu4[...] = pick(table, mine >> 6)
    tall = jnp.concatenate([pick(table, mine & 63)] * 4, axis=0)
    ahead = lax.broadcasted_iota(jnp.int32, (256, 128), 0) // 64
    along = lax.broadcasted_iota(jnp.int32, (256, 128), 1) // 32
    high, low = split(jnp.where(ahead == along, tall, f32(0)))
    bhl[:, :128] = high
    bhl[:, 128:] = low
    bhh[:, :128] = high
    bhh[:, 128:] = high

    for slot in range(4):
        x_copies[slot].wait()

        @pl.loop(0, 8)
        def _(n):
            a = slot * 8 + n
            high, low = split(but[pl.ds(a, 1), :] * bvt[...])
            to = pl.ds(pl.multiple_of(a * CH, CH), CH)
            eh_ref[to, :] = high
            el_ref[to, :] = low
            at = pl.ds(pl.multiple_of(n * 256, 256), 256)
            xt[slot, at, :] = xv[slot * 256 : slot * 256 + 256, at].T

        if slot == 1:
            forward(0)
            for cp in sends[1][2:4] + w_copies:
                cp.start()

    gone = []

    def send(h, dst, sem, at, to):
        cp = pltpu.make_async_remote_copy(
            src_ref=own_ref.at[h, at],
            dst_ref=dst.at[h, at],
            send_sem=c_send.at[len(gone)],
            recv_sem=sem.at[h * 16 + at],
            device_id={"rep": to},
        )
        cp.start()
        gone.append(cp)

    def arrived(h, ref, sem, at):
        pltpu.make_async_remote_copy(
            src_ref=ref.at[h, at], dst_ref=ref.at[h, at], send_sem=c_send.at[0], recv_sem=sem.at[h * 16 + at],
            device_id={"rep": partner},
        ).wait_recv()

    def pass_on(h, n0, n1):
        for dy, dz in offsets()[n0:n1]:
            at = chip_at(-dy, -dz)
            arrived(h, own_ref, own_recv, at)
            send(h, oth_ref, oth_recv, at, partner)

    def momentum(h):
        own_g[h].wait()
        sends[h][2].wait_recv()
        sends[h][3].wait_recv()
        if h == 0:
            m_copy.wait()
        cols = slice(h * 256, h * 256 + 256)
        for n in range(4):
            at = slice(n * 512, n * 512 + 512)
            lhs = jnp.concatenate([xt[s, at, :] for s in range(3)], axis=1)
            part = dot(lhs, gv[h, 0:768, :], NN) * f32(1.0 / 1024)
            m_ref[at, cols] = f32(MOMENTUM_DECAY) * m_ref[at, cols] + part

    def coefficients(h):
        sends[h][4].wait_recv()
        sends[h][5].wait_recv()
        cols = slice(h * 256, h * 256 + 256)
        for n in range(4):
            at = slice(n * 512, n * 512 + 512)
            value = m_ref[at, cols] + dot(xt[3, at, :], gv[h, 768:1024, :], NN) * f32(1.0 / 1024)
            m_ref[at, cols] = value
            high, low = split(value)
            wide = dot(high, bhl[...], NN)
            inner = wide[:, :128] + wide[:, 128:] + dot(low, bhl[:, :128], NN)
            cown[h, n * 8 : n * 8 + 8, :] = jnp.sum(inner.reshape(8, CH, 128) * bu4[...][None], axis=1)
        turned = cown[h].T
        own_ref[h, chip] = jnp.concatenate([turned[j * 32 : j * 32 + 32, :] for j in range(4)], axis=1)
        for dy, dz in offsets()[::-1]:
            send(h, own_ref, own_recv, chip, chip_at(dy, dz) * 2 + core)
        send(h, oth_ref, oth_recv, chip, partner)

    forward(1)
    momentum(0)
    coefficients(0)
    momentum(1)
    coefficients(1)

    def take_away(h):
        for n in range(4):
            at, cols = slice(n * 512, n * 512 + 512), slice(h * 256, h * 256 + 256)
            field = cown[h, n * 8 : n * 8 + 8, :][:, None, :] * bu4[...][None]
            high, low = split(field.reshape(512, 128))
            back = dot(jnp.concatenate([high, low], axis=1), bhh[...], NT) + dot(high, bhl[:, 128:], NT)
            m_ref[at, cols] = m_ref[at, cols] - back

    rows = [pl.ds(pl.multiple_of(b * 256, 256), 256) for b in blocks]
    pass_on(0, 0, 8)
    take_away(0)
    take_away(1)
    pass_on(0, 8, 15)
    for cp in w_copies:
        cp.wait()
    input_grad(0, wv, gv, grad_ref, rows, 0)
    pass_on(1, 0, 4)
    input_grad(1, wv, gv, grad_ref, rows, 1)
    pass_on(1, 4, 10)
    for n in range(16):
        arrived(0, oth_ref, oth_recv, n)
    fill(0, own_ref, oth_ref, sign_ref, lh, ll)
    decode(0, 0, eh_ref, el_ref, lh, ll, wv, nw)
    pass_on(1, 10, 15)
    for n in range(1, 4):
        decode(0, n, eh_ref, el_ref, lh, ll, wv, nw)
    for n in range(16):
        arrived(1, oth_ref, oth_recv, n)
    for cp in sends[0] + sends[1] + gone:
        cp.wait_send()


def input_grad(n, wv, gv, to, rows, place):
    part = None
    for h in range(2):
        pair = [wv[2 * h + k, n * 8 : n * 8 + 8].reshape(512, 128) for k in range(2)]
        high, low = split(jnp.concatenate(pair, axis=1))
        new = dot(gv[h], high, NT) + dot(gv[h], low, NT)
        part = new if part is None else part + new
    for s in range(4):
        to[rows[s], place * 512 : place * 512 + 512] = part[s * 256 : s * 256 + 256, :]


def fill(h, own_ref, oth_ref, sign_ref, lh, ll):
    both = jnp.concatenate([own_ref[h].reshape(512, 128), oth_ref[h].reshape(512, 128)], axis=0)
    turned = both.T * f32(STEP_RATE)
    mirrored = turned * sign_ref[0:1, :]
    high, low = split(jnp.concatenate([turned, mirrored], axis=0))
    lh[...] = high
    ll[...] = low


def decode(h, n, eh_ref, el_ref, lh, ll, w_ref, nw):
    low_half = lax.broadcasted_iota(jnp.int32, (32, 128), 1) < 64
    at = slice(n * 512, n * 512 + 512)
    eh = eh_ref[at, :]
    total = dot(lh[...], eh, NT) + dot(ll[...], eh, NT) + dot(lh[...], el_ref[at, :], NT)
    for side in range(2):
        for j in range(2):
            vals = []
            for k in range(4):
                top = side * 128 + j * 64
                one = total[top : top + 32, k * 128 : k * 128 + 128]
                two = total[top + 32 : top + 64, k * 128 : k * 128 + 128]
                vals.append(jnp.where(low_half, one, pltpu.roll(two, 64, 1)))
                vals.append(jnp.where(low_half, pltpu.roll(one, 64, 1), two))
            first = 56 - 8 * n if side else 8 * n
            if side:
                vals = vals[::-1]
            rows = slice(first, first + 8)
            nw[j, :, rows, :] = w_ref[2 * h + j, :, rows, :] - jnp.swapaxes(jnp.stack(vals, axis=0), 0, 1)


def second_kernel(
    m_ref, grad_ref, eh_ref, el_ref, sign_ref, own_ref, oth_ref, new_ref, w_ref, gv,
    grad_hbm, res_hbm, new_hbm, rest, nw, lh, ll, sems,
):
    feat = lax.axis_index("feat")
    blocks = (feat, (feat + 3) % 4, (feat + 1) % 4, (feat + 2) % 4)
    rows = [pl.ds(pl.multiple_of(b * 256, 256), 256) for b in blocks]
    copies = []

    def start(src, dst):
        cp = pltpu.make_async_copy(src, dst, sems.at[len(copies)])
        cp.start()
        copies.append(cp)

    start(grad_ref, grad_hbm.at[:, pl.ds(0, 1024)])
    start(m_ref, res_hbm)
    for j in range(2):
        start(new_ref.at[j], new_hbm.at[:, :, pl.ds(j * 128, 128)])
    for n in range(2):
        input_grad(2 + n, w_ref, gv, rest, rows, n)
        start(rest.at[:, pl.ds(n * 512, 512)], grad_hbm.at[:, pl.ds(1024 + n * 512, 512)])
    fill(1, own_ref, oth_ref, sign_ref, lh, ll)
    for n in range(4):
        decode(1, n, eh_ref, el_ref, lh, ll, w_ref, nw)
        for first in (8 * n, 56 - 8 * n):
            for j in range(2):
                part = pl.ds(first, 8)
                start(nw.at[j, :, part], new_hbm.at[:, part, pl.ds(256 + j * 128, 128)])
    for cp in copies:
        cp.wait()


def vmem(shape, dtype):
    return pltpu.VMEM(shape, dtype)


def body(x, g, w, mom, sel):
    any_space = pl.BlockSpec(memory_space=pl.ANY)
    vm = pl.BlockSpec(memory_space=pltpu.VMEM)
    mid = pl.pallas_call(
        first_kernel,
        out_shape=(
            vmem((2048, 512), f32),
            vmem((1024, 1024), f32),
            vmem((2048, 1024), bf16),
            vmem((2048, 1024), bf16),
            vmem((8, 1024), f32),
            vmem((2, 16, 32, 128), f32),
            vmem((2, 16, 32, 128), f32),
            vmem((2, 32, CH, 128), f32),
            vmem((4, 32, CH, 128), f32),
            vmem((2, 1024, 256), bf16),
        ),
        in_specs=[any_space] * 5,
        out_specs=[vm] * 10,
        scratch_shapes=[
            pltpu.VMEM((1024, 2048), bf16),
            pltpu.VMEM((4, 2048, 256), bf16),
            pltpu.VMEM((32, 32), jnp.int32),
            pltpu.VMEM((CH, 1024), f32),
            pltpu.VMEM((CH, 1024), f32),
            pltpu.VMEM((256, 256), bf16),
            pltpu.VMEM((256, 256), bf16),
            pltpu.VMEM((CH, 128), f32),
            pltpu.VMEM((2, 32, 128), f32),
            pltpu.VMEM((256, 1024), bf16),
            pltpu.VMEM((256, 1024), bf16),
            pltpu.SemaphoreType.DMA((12,)),
            pltpu.SemaphoreType.DMA((12,)),
            pltpu.SemaphoreType.DMA((12,)),
            pltpu.SemaphoreType.DMA((62,)),
            pltpu.SemaphoreType.DMA((32,)),
            pltpu.SemaphoreType.DMA((32,)),
        ],
        compiler_params=pltpu.CompilerParams(
            collective_id=0, has_side_effects=True, vmem_limit_bytes=18 * MIB
        ),
        name="gather_and_select",
    )(*(pltpu.with_memory_space_constraint(v, pltpu.HBM) for v in (x, g, w.reshape(32, CH, 512), mom[0], sel)))
    grad, res, new = pl.pallas_call(
        second_kernel,
        out_shape=(
            jax.ShapeDtypeStruct((1024, 2048), f32),
            jax.ShapeDtypeStruct((2048, 512), f32),
            jax.ShapeDtypeStruct((32, CH, 512), f32),
        ),
        in_specs=[vm] * 10,
        out_specs=[any_space] * 3,
        scratch_shapes=[
            pltpu.VMEM((1024, 1024), f32),
            pltpu.VMEM((2, 32, CH, 128), f32),
            pltpu.VMEM((256, 1024), bf16),
            pltpu.VMEM((256, 1024), bf16),
            pltpu.SemaphoreType.DMA((22,)),
        ],
        compiler_params=pltpu.CompilerParams(vmem_limit_bytes=14 * MIB),
        name="decode_and_write",
    )(*(pltpu.with_memory_space_constraint(v, pltpu.VMEM) for v in mid))
    return grad, res[None], new.reshape(2048, 512)


def solution(mesh):
    in_specs = (P("rep", "feat"), P(("rep", "feat"), None), P("feat", None), P("rep", "feat", None), P())
    out_specs = (P("rep", "feat"), P("rep", "feat", None), P("feat", None))
    return jax.shard_map(body, mesh=mesh, in_specs=in_specs, out_specs=out_specs, check_vma=False)
```

```python
import functools

import jax
import jax.numpy as jnp
from jax import lax
from jax.experimental import pallas as pl
from jax.experimental.pallas import tpu as pltpu
from jax.sharding import PartitionSpec as P

CH = 64
MOMENTUM_DECAY = 0.9
STEP_RATE = 0.5
f32 = jnp.float32
bf16 = jnp.bfloat16
NN = (((1,), (0,)), ((), ()))
NT = (((1,), (1,)), ((), ()))
TN = (((0,), (0,)), ((), ()))
MIB = 1 << 20


def dot(a, b, dims, precision=None):
    return lax.dot_general(a, b, dims, precision=precision, preferred_element_type=f32)


def split(v):
    high = v.astype(bf16)
    return high, (v - high.astype(f32)).astype(bf16)


def dct_transposed():
    a = lax.broadcasted_iota(jnp.int32, (CH, CH), 0)
    u = lax.broadcasted_iota(jnp.int32, (CH, CH), 1)
    turn = ((2 * a + 1) * u) & 255
    table = jnp.cos(turn.astype(f32) * f32(jnp.pi / 128)) * f32((2.0 / CH) ** 0.5)
    return jnp.where(u == 0, f32((1.0 / CH) ** 0.5), table)


def pick(table, row):
    n = row.shape[1]
    hot = (lax.broadcasted_iota(jnp.int32, (CH, n), 0) == jnp.broadcast_to(row, (CH, n))).astype(f32)
    return dot(table, hot, NN, lax.Precision.HIGHEST)


def offsets():
    both = [(dy, dz) for dy in range(4) for dz in range(4) if (dy, dz) != (0, 0)]
    return sorted(both, key=lambda o: (min(o[0], 4 - o[0]) + min(o[1], 4 - o[1]), o))


def first_kernel(
    x_hbm, g_hbm, w_hbm, mom_hbm, sel_hbm,
    m_ref, grad_ref, eh_ref, el_ref, sign_ref, own_ref, oth_ref, nw, wv, gv,
    xv, xt, sel_ref, but, bvt, bhl, bhh, bu4, cown, lh, ll, acc,
    local_sem, g_send, g_recv, c_send, own_recv, oth_recv,
):
    feat = lax.axis_index("feat")
    rep = lax.axis_index("rep")
    core = rep % 2
    chip = rep // 2
    y, z = chip // 4, chip % 4
    partner = rep + 1 - 2 * core
    right, left, across = (feat + 1) % 4, (feat + 3) % 4, (feat + 2) % 4
    blocks = (feat, left, right, across)

    def chip_at(dy, dz):
        return (y + dy) % 4 * 4 + (z + dz) % 4

    barrier = pltpu.get_barrier_semaphore()
    for f in (left, right):
        pl.semaphore_signal(barrier, inc=1, device_id={"feat": f})
    for dy, dz in offsets():
        pl.semaphore_signal(barrier, inc=1, device_id={"rep": chip_at(dy, dz) * 2 + core})
        pl.semaphore_signal(barrier, inc=1, device_id={"rep": chip_at(dy, dz) * 2 + 1 - core})
    pl.semaphore_signal(barrier, inc=1, device_id={"rep": partner})

    sel_copy = pltpu.make_async_copy(sel_hbm, sel_ref, local_sem.at[0])
    own_g = [
        pltpu.make_async_copy(g_hbm.at[:, pl.ds(h * 256, 256)], gv.at[h, pl.ds(0, 256)], local_sem.at[1 + h])
        for h in range(2)
    ]
    x_copies = [
        pltpu.make_async_copy(x_hbm.at[pl.ds(b * 256, 256)], xv.at[pl.ds(n * 256, 256)], local_sem.at[3 + n])
        for n, b in enumerate(blocks)
    ]
    m_copy = pltpu.make_async_copy(mom_hbm, m_ref, local_sem.at[7])
    w_copies = [
        pltpu.make_async_copy(w_hbm.at[:, :, pl.ds(n * 128, 128)], wv.at[n], local_sem.at[8 + n]) for n in range(4)
    ]
    for cp in [sel_copy] + x_copies:
        cp.start()

    def g_copy(h, n, slot, half, to, forward=None):
        if forward is None:
            src = g_hbm.at[pl.ds(half * 128, 128), pl.ds(h * 256, 256)]
        else:
            src = gv.at[h, pl.ds(forward * 256 + half * 128, 128)]
        return pltpu.make_async_remote_copy(
            src_ref=src,
            dst_ref=gv.at[h, pl.ds(slot * 256 + half * 128, 128)],
            send_sem=g_send.at[h * 6 + n],
            recv_sem=g_recv.at[h * 6 + n],
            device_id={"feat": to},
        )

    sends = [
        [
            g_copy(h, 0, 1, 0, right),
            g_copy(h, 1, 2, 1, left),
            g_copy(h, 2, 1, 1, right),
            g_copy(h, 3, 2, 0, left),
            g_copy(h, 4, 3, 0, right, 1),
            g_copy(h, 5, 3, 1, left, 2),
        ]
        for h in range(2)
    ]
    pl.semaphore_wait(barrier, 33)
    for cp in sends[0][:4] + sends[1][:2]:
        cp.start()

    def forward(h):
        for n in range(2):
            sends[h][n].wait_recv()
            sends[h][4 + n].start()

    table = dct_transposed()
    sel_copy.wait()
    for cp in own_g + [m_copy]:
        cp.start()
    rows = []
    for s in range(32):
        plane = core if s < 16 else 1 - core
        rows.append(sel_ref[pl.ds((s % 16) * 2 + plane, 1), :])
    flat = jnp.concatenate(rows, axis=1)
    but[...] = pick(table, flat >> 6)
    bvt[...] = pick(table, flat & 63)
    sign_ref[...] = jnp.broadcast_to(f32(1) - f32(2) * ((flat >> 6) & 1).astype(f32), (8, 1024))
    mine = sel_ref[pl.ds(rep, 1), :]
    mine = jnp.concatenate([mine] * 4, axis=1)
    bu4[...] = pick(table, mine >> 6)
    tall = jnp.concatenate([pick(table, mine & 63)] * 4, axis=0)
    ahead = lax.broadcasted_iota(jnp.int32, (256, 128), 0) // 64
    along = lax.broadcasted_iota(jnp.int32, (256, 128), 1) // 32
    high, low = split(jnp.where(ahead == along, tall, f32(0)))
    bhl[:, :128] = high
    bhl[:, 128:] = low
    bhh[:, :128] = high
    bhh[:, 128:] = high

    for slot in range(4):
        x_copies[slot].wait()

        @pl.loop(0, 8)
        def _(n):
            at = pl.ds(pl.multiple_of(n * 256, 256), 256)
            xt[slot, at, :] = xv[slot * 256 : slot * 256 + 256, at].T

        if slot == 3:
            forward(0)
            for cp in sends[1][2:4] + w_copies:
                cp.start()

    def outer(first, last):
        @pl.loop(first, last)
        def _(a):
            high, low = split(but[pl.ds(a, 1), :] * bvt[...])
            to = pl.ds(pl.multiple_of(a * CH, CH), CH)
            eh_ref[to, :] = high
            el_ref[to, :] = low

    gone = []

    def send(h, dst, sem, at, to):
        cp = pltpu.make_async_remote_copy(
            src_ref=own_ref.at[h, at],
            dst_ref=dst.at[h, at],
            send_sem=c_send.at[len(gone)],
            recv_sem=sem.at[h * 16 + at],
            device_id={"rep": to},
        )
        cp.start()
        gone.append(cp)

    def arrived(h, ref, sem, at):
        pltpu.make_async_remote_copy(
            src_ref=ref.at[h, at], dst_ref=ref.at[h, at], send_sem=c_send.at[0], recv_sem=sem.at[h * 16 + at],
            device_id={"rep": partner},
        ).wait_recv()

    def pass_on(h, n0, n1):
        for dy, dz in offsets()[n0:n1]:
            at = chip_at(-dy, -dz)
            arrived(h, own_ref, own_recv, at)
            send(h, oth_ref, oth_recv, at, partner)

    def momentum(h):
        own_g[h].wait()
        sends[h][2].wait_recv()
        sends[h][3].wait_recv()
        if h == 0:
            m_copy.wait()
        cols = slice(h * 256, h * 256 + 256)
        for n in range(4):
            at = slice(n * 512, n * 512 + 512)
            lhs = jnp.concatenate([xt[s, at, :] for s in range(3)], axis=1)
            part = dot(lhs, gv[h, 0:768, :], NN) * f32(1.0 / 1024)
            m_ref[at, cols] = f32(MOMENTUM_DECAY) * m_ref[at, cols] + part

    def coefficients(h):
        sends[h][4].wait_recv()
        sends[h][5].wait_recv()
        cols = slice(h * 256, h * 256 + 256)
        for n in range(4):
            at = slice(n * 512, n * 512 + 512)
            value = m_ref[at, cols] + dot(xt[3, at, :], gv[h, 768:1024, :], NN) * f32(1.0 / 1024)
            m_ref[at, cols] = value
            high, low = split(value)
            wide = dot(high, bhl[...], NN)
            inner = wide[:, :128] + wide[:, 128:] + dot(low, bhl[:, :128], NN)
            cown[h, n * 8 : n * 8 + 8, :] = jnp.sum(inner.reshape(8, CH, 128) * bu4[...][None], axis=1)
        turned = cown[h].T
        own_ref[h, chip] = jnp.concatenate([turned[j * 32 : j * 32 + 32, :] for j in range(4)], axis=1)
        for dy, dz in offsets()[::-1]:
            send(h, own_ref, own_recv, chip, chip_at(dy, dz) * 2 + core)
            if h == 1:
                send(h, oth_ref, oth_recv, chip, chip_at(dy, dz) * 2 + 1 - core)
        send(h, oth_ref, oth_recv, chip, partner)

    outer(0, 8)
    momentum(0)
    forward(1)
    outer(8, 32)
    coefficients(0)
    momentum(1)
    coefficients(1)

    def take_away(h):
        for n in range(4):
            at, cols = slice(n * 512, n * 512 + 512), slice(h * 256, h * 256 + 256)
            field = cown[h, n * 8 : n * 8 + 8, :][:, None, :] * bu4[...][None]
            high, low = split(field.reshape(512, 128))
            back = dot(jnp.concatenate([high, low], axis=1), bhh[...], NT) + dot(high, bhl[:, 128:], NT)
            m_ref[at, cols] = m_ref[at, cols] - back

    rows = [pl.ds(pl.multiple_of(b * 256, 256), 256) for b in blocks]
    take_away(0)
    take_away(1)
    pass_on(0, 0, 8)
    for cp in w_copies:
        cp.wait()
    input_grad(0, wv, gv, grad_ref, rows, 0)
    pass_on(0, 8, 15)
    fill(own_ref, 0, 0, sign_ref, lh, ll)
    acc[:, 0:512] = product(0, 0, 512, eh_ref, el_ref, lh, ll)
    acc[:, 512:1024] = product(1, 0, 512, eh_ref, el_ref, lh, ll)
    acc[:, 1024:1536] = product(2, 0, 512, eh_ref, el_ref, lh, ll)
    acc[:, 1536:2048] = product(3, 0, 512, eh_ref, el_ref, lh, ll)
    input_grad(1, wv, gv, grad_ref, rows, 1)
    for n in range(16):
        arrived(0, oth_ref, oth_recv, n)
    fill(oth_ref, 0, 1, sign_ref, lh, ll)
    for n in range(4):
        total = acc[:, n * 512 : n * 512 + 512] + product(n, 512, 1024, eh_ref, el_ref, lh, ll)
        place(0, n, total, wv, nw)
    for dy, dz in offsets():
        arrived(1, own_ref, own_recv, chip_at(-dy, -dz))
    for n in range(16):
        arrived(1, oth_ref, oth_recv, n)
    for cp in sends[0] + sends[1] + gone:
        cp.wait_send()


def input_grad(n, wv, gv, to, rows, place):
    part = None
    for h in range(2):
        pair = [wv[2 * h + k, n * 8 : n * 8 + 8].reshape(512, 128) for k in range(2)]
        high, low = split(jnp.concatenate(pair, axis=1))
        new = dot(gv[h], high, NT) + dot(gv[h], low, NT)
        part = new if part is None else part + new
    for s in range(4):
        to[rows[s], place * 512 : place * 512 + 512] = part[s * 256 : s * 256 + 256, :]


def fill(ref, h, half, sign_ref, lh, ll):
    at = slice(half * 512, half * 512 + 512)
    turned = ref[h].reshape(512, 128).T * f32(STEP_RATE)
    high, low = split(jnp.concatenate([turned, turned * sign_ref[0:1, at]], axis=0))
    lh[:, at] = high
    ll[:, at] = low


def product(n, first, last, eh_ref, el_ref, lh, ll):
    at, terms = slice(n * 512, n * 512 + 512), slice(first, last)
    high, low, eh = lh[:, terms], ll[:, terms], eh_ref[at, terms]
    return dot(high, eh, NT) + dot(low, eh, NT) + dot(high, el_ref[at, terms], NT)


def place(h, n, total, w_ref, nw):
    low_half = lax.broadcasted_iota(jnp.int32, (32, 128), 1) < 64
    for side in range(2):
        for j in range(2):
            vals = []
            for k in range(4):
                top = side * 128 + j * 64
                one = total[top : top + 32, k * 128 : k * 128 + 128]
                two = total[top + 32 : top + 64, k * 128 : k * 128 + 128]
                vals.append(jnp.where(low_half, one, pltpu.roll(two, 64, 1)))
                vals.append(jnp.where(low_half, pltpu.roll(one, 64, 1), two))
            first = 56 - 8 * n if side else 8 * n
            if side:
                vals = vals[::-1]
            rows = slice(first, first + 8)
            nw[j, :, rows, :] = w_ref[2 * h + j, :, rows, :] - jnp.swapaxes(jnp.stack(vals, axis=0), 0, 1)


def second_kernel(
    m_ref, grad_ref, eh_ref, el_ref, sign_ref, own_ref, oth_ref, new_ref, w_ref, gv,
    grad_hbm, res_hbm, new_hbm, rest, nw, lh, ll, sems,
):
    feat = lax.axis_index("feat")
    blocks = (feat, (feat + 3) % 4, (feat + 1) % 4, (feat + 2) % 4)
    rows = [pl.ds(pl.multiple_of(b * 256, 256), 256) for b in blocks]
    copies = []

    def start(src, dst):
        cp = pltpu.make_async_copy(src, dst, sems.at[len(copies)])
        cp.start()
        copies.append(cp)

    start(grad_ref, grad_hbm.at[:, pl.ds(0, 1024)])
    start(m_ref, res_hbm)
    for j in range(2):
        start(new_ref.at[j], new_hbm.at[:, :, pl.ds(j * 128, 128)])
    for n in range(2):
        input_grad(2 + n, w_ref, gv, rest, rows, n)
        start(rest.at[:, pl.ds(n * 512, 512)], grad_hbm.at[:, pl.ds(1024 + n * 512, 512)])
    fill(own_ref, 1, 0, sign_ref, lh, ll)
    fill(oth_ref, 1, 1, sign_ref, lh, ll)
    for n in range(4):
        place(1, n, product(n, 0, 1024, eh_ref, el_ref, lh, ll), w_ref, nw)
        for first in (8 * n, 56 - 8 * n):
            for j in range(2):
                part = pl.ds(first, 8)
                start(nw.at[j, :, part], new_hbm.at[:, part, pl.ds(256 + j * 128, 128)])
    for cp in copies:
        cp.wait()


def vmem(shape, dtype):
    return pltpu.VMEM(shape, dtype)


def body(x, g, w, mom, sel):
    any_space = pl.BlockSpec(memory_space=pl.ANY)
    vm = pl.BlockSpec(memory_space=pltpu.VMEM)
    mid = pl.pallas_call(
        first_kernel,
        out_shape=(
            vmem((2048, 512), f32),
            vmem((1024, 1024), f32),
            vmem((2048, 1024), bf16),
            vmem((2048, 1024), bf16),
            vmem((8, 1024), f32),
            vmem((2, 16, 32, 128), f32),
            vmem((2, 16, 32, 128), f32),
            vmem((2, 32, CH, 128), f32),
            vmem((4, 32, CH, 128), f32),
            vmem((2, 1024, 256), bf16),
        ),
        in_specs=[any_space] * 5,
        out_specs=[vm] * 10,
        scratch_shapes=[
            pltpu.VMEM((1024, 2048), bf16),
            pltpu.VMEM((4, 2048, 256), bf16),
            pltpu.VMEM((32, 32), jnp.int32),
            pltpu.VMEM((CH, 1024), f32),
            pltpu.VMEM((CH, 1024), f32),
            pltpu.VMEM((256, 256), bf16),
            pltpu.VMEM((256, 256), bf16),
            pltpu.VMEM((CH, 128), f32),
            pltpu.VMEM((2, 32, 128), f32),
            pltpu.VMEM((256, 1024), bf16),
            pltpu.VMEM((256, 1024), bf16),
            pltpu.VMEM((256, 2048), f32),
            pltpu.SemaphoreType.DMA((12,)),
            pltpu.SemaphoreType.DMA((12,)),
            pltpu.SemaphoreType.DMA((12,)),
            pltpu.SemaphoreType.DMA((62,)),
            pltpu.SemaphoreType.DMA((32,)),
            pltpu.SemaphoreType.DMA((32,)),
        ],
        compiler_params=pltpu.CompilerParams(
            collective_id=0, has_side_effects=True, vmem_limit_bytes=18 * MIB
        ),
        name="gather_and_select",
    )(*(pltpu.with_memory_space_constraint(v, pltpu.HBM) for v in (x, g, w.reshape(32, CH, 512), mom[0], sel)))
    grad, res, new = pl.pallas_call(
        second_kernel,
        out_shape=(
            jax.ShapeDtypeStruct((1024, 2048), f32),
            jax.ShapeDtypeStruct((2048, 512), f32),
            jax.ShapeDtypeStruct((32, CH, 512), f32),
        ),
        in_specs=[vm] * 10,
        out_specs=[any_space] * 3,
        scratch_shapes=[
            pltpu.VMEM((1024, 1024), f32),
            pltpu.VMEM((2, 32, CH, 128), f32),
            pltpu.VMEM((256, 1024), bf16),
            pltpu.VMEM((256, 1024), bf16),
            pltpu.SemaphoreType.DMA((22,)),
        ],
        compiler_params=pltpu.CompilerParams(vmem_limit_bytes=14 * MIB),
        name="decode_and_write",
    )(*(pltpu.with_memory_space_constraint(v, pltpu.VMEM) for v in mid))
    return grad, res[None], new.reshape(2048, 512)


def solution(mesh):
    in_specs = (P("rep", "feat"), P(("rep", "feat"), None), P("feat", None), P("rep", "feat", None), P())
    out_specs = (P("rep", "feat"), P("rep", "feat", None), P("feat", None))
    return jax.shard_map(body, mesh=mesh, in_specs=in_specs, out_specs=out_specs, check_vma=False)
```

```python
import functools

import jax
import jax.numpy as jnp
from jax import lax
from jax.experimental import pallas as pl
from jax.experimental.pallas import tpu as pltpu
from jax.sharding import PartitionSpec as P

CH = 64
MOMENTUM_DECAY = 0.9
STEP_RATE = 0.5
f32 = jnp.float32
bf16 = jnp.bfloat16
NN = (((1,), (0,)), ((), ()))
NT = (((1,), (1,)), ((), ()))
TN = (((0,), (0,)), ((), ()))
MIB = 1 << 20


def dot(a, b, dims, precision=None):
    return lax.dot_general(a, b, dims, precision=precision, preferred_element_type=f32)


def split(v):
    high = v.astype(bf16)
    return high, (v - high.astype(f32)).astype(bf16)


def dct_transposed():
    a = lax.broadcasted_iota(jnp.int32, (CH, CH), 0)
    u = lax.broadcasted_iota(jnp.int32, (CH, CH), 1)
    turn = ((2 * a + 1) * u) & 255
    table = jnp.cos(turn.astype(f32) * f32(jnp.pi / 128)) * f32((2.0 / CH) ** 0.5)
    return jnp.where(u == 0, f32((1.0 / CH) ** 0.5), table)


def pick(table, row):
    n = row.shape[1]
    hot = (lax.broadcasted_iota(jnp.int32, (CH, n), 0) == jnp.broadcast_to(row, (CH, n))).astype(f32)
    return dot(table, hot, NN, lax.Precision.HIGHEST)


def offsets():
    both = [(dy, dz) for dy in range(4) for dz in range(4) if (dy, dz) != (0, 0)]
    return sorted(both, key=lambda o: (min(o[0], 4 - o[0]) + min(o[1], 4 - o[1]), o))


def first_kernel(
    x_hbm, g_hbm, w_hbm, mom_hbm, sel_hbm,
    m_ref, grad_ref, eh_ref, el_ref, sign_ref, own_ref, oth_ref, nw, wv, gv,
    xv, xt, sel_ref, but, bvt, bhl, bhh, bu4, cown, lh, ll, acc,
    local_sem, g_send, g_recv, c_send, own_recv, oth_recv,
):
    feat = lax.axis_index("feat")
    rep = lax.axis_index("rep")
    core = rep % 2
    chip = rep // 2
    y, z = chip // 4, chip % 4
    partner = rep + 1 - 2 * core
    right, left, across = (feat + 1) % 4, (feat + 3) % 4, (feat + 2) % 4
    blocks = (feat, left, right, across)

    def chip_at(dy, dz):
        return (y + dy) % 4 * 4 + (z + dz) % 4

    barrier = pltpu.get_barrier_semaphore()
    for f in (left, right):
        pl.semaphore_signal(barrier, inc=1, device_id={"feat": f})
    for dy, dz in offsets():
        pl.semaphore_signal(barrier, inc=1, device_id={"rep": chip_at(dy, dz) * 2 + core})
        pl.semaphore_signal(barrier, inc=1, device_id={"rep": chip_at(dy, dz) * 2 + 1 - core})
    pl.semaphore_signal(barrier, inc=1, device_id={"rep": partner})

    sel_copy = pltpu.make_async_copy(sel_hbm, sel_ref, local_sem.at[0])
    own_g = [
        pltpu.make_async_copy(g_hbm.at[:, pl.ds(h * 256, 256)], gv.at[h, pl.ds(0, 256)], local_sem.at[1 + h])
        for h in range(2)
    ]
    x_copies = [
        pltpu.make_async_copy(x_hbm.at[pl.ds(b * 256, 256)], xv.at[pl.ds(n * 256, 256)], local_sem.at[3 + n])
        for n, b in enumerate(blocks)
    ]
    m_copy = pltpu.make_async_copy(mom_hbm, m_ref, local_sem.at[7])
    w_copies = [
        pltpu.make_async_copy(w_hbm.at[:, :, pl.ds(n * 128, 128)], wv.at[n], local_sem.at[8 + n]) for n in range(4)
    ]
    for cp in [sel_copy] + x_copies:
        cp.start()

    def g_copy(h, n, slot, half, to, forward=None):
        if forward is None:
            src = g_hbm.at[pl.ds(half * 128, 128), pl.ds(h * 256, 256)]
        else:
            src = gv.at[h, pl.ds(forward * 256 + half * 128, 128)]
        return pltpu.make_async_remote_copy(
            src_ref=src,
            dst_ref=gv.at[h, pl.ds(slot * 256 + half * 128, 128)],
            send_sem=g_send.at[h * 6 + n],
            recv_sem=g_recv.at[h * 6 + n],
            device_id={"feat": to},
        )

    sends = [
        [
            g_copy(h, 0, 1, 0, right),
            g_copy(h, 1, 2, 1, left),
            g_copy(h, 2, 1, 1, right),
            g_copy(h, 3, 2, 0, left),
            g_copy(h, 4, 3, 0, right, 1),
            g_copy(h, 5, 3, 1, left, 2),
        ]
        for h in range(2)
    ]
    pl.semaphore_wait(barrier, 33)
    for cp in sends[0][:4] + sends[1][:2]:
        cp.start()

    def forward(h):
        for n in range(2):
            sends[h][n].wait_recv()
            sends[h][4 + n].start()

    table = dct_transposed()
    sel_copy.wait()
    for cp in own_g + [m_copy]:
        cp.start()
    rows = []
    for s in range(32):
        plane = core if s < 16 else 1 - core
        rows.append(sel_ref[pl.ds((s % 16) * 2 + plane, 1), :])
    flat = jnp.concatenate(rows, axis=1)
    but[...] = pick(table, flat >> 6)
    bvt[...] = pick(table, flat & 63)
    sign_ref[...] = jnp.broadcast_to(f32(1) - f32(2) * ((flat >> 6) & 1).astype(f32), (8, 1024))
    mine = sel_ref[pl.ds(rep, 1), :]
    mine = jnp.concatenate([mine] * 4, axis=1)
    bu4[...] = pick(table, mine >> 6)
    tall = jnp.concatenate([pick(table, mine & 63)] * 4, axis=0)
    ahead = lax.broadcasted_iota(jnp.int32, (256, 128), 0) // 64
    along = lax.broadcasted_iota(jnp.int32, (256, 128), 1) // 32
    high, low = split(jnp.where(ahead == along, tall, f32(0)))
    bhl[:, :128] = high
    bhl[:, 128:] = low
    bhh[:, :128] = high
    bhh[:, 128:] = high

    for slot in range(4):
        x_copies[slot].wait()

        @pl.loop(0, 8)
        def _(n):
            at = pl.ds(pl.multiple_of(n * 256, 256), 256)
            xt[slot, at, :] = xv[slot * 256 : slot * 256 + 256, at].T

        if slot == 3:
            forward(0)
            for cp in sends[1][2:4] + w_copies:
                cp.start()

    def outer(first, last):
        @pl.loop(first, last)
        def _(a):
            high, low = split(but[pl.ds(a, 1), :] * bvt[...])
            to = pl.ds(pl.multiple_of(a * CH, CH), CH)
            eh_ref[to, :] = high
            el_ref[to, :] = low

    gone = []

    def send(h, dst, sem, at, to):
        cp = pltpu.make_async_remote_copy(
            src_ref=own_ref.at[h, at],
            dst_ref=dst.at[h, at],
            send_sem=c_send.at[len(gone)],
            recv_sem=sem.at[h * 16 + at],
            device_id={"rep": to},
        )
        cp.start()
        gone.append(cp)

    def arrived(h, ref, sem, at):
        pltpu.make_async_remote_copy(
            src_ref=ref.at[h, at], dst_ref=ref.at[h, at], send_sem=c_send.at[0], recv_sem=sem.at[h * 16 + at],
            device_id={"rep": partner},
        ).wait_recv()

    def pass_on(h, n0, n1):
        for dy, dz in offsets()[n0:n1]:
            at = chip_at(-dy, -dz)
            arrived(h, own_ref, own_recv, at)
            send(h, oth_ref, oth_recv, at, partner)

    def momentum(h):
        own_g[h].wait()
        sends[h][2].wait_recv()
        sends[h][3].wait_recv()
        if h == 0:
            m_copy.wait()
        cols = slice(h * 256, h * 256 + 256)
        for n in range(4):
            at = slice(n * 512, n * 512 + 512)
            lhs = jnp.concatenate([xt[s, at, :] for s in range(3)], axis=1)
            part = dot(lhs, gv[h, 0:768, :], NN) * f32(1.0 / 1024)
            m_ref[at, cols] = f32(MOMENTUM_DECAY) * m_ref[at, cols] + part

    def coefficients(h):
        sends[h][4].wait_recv()
        sends[h][5].wait_recv()
        cols = slice(h * 256, h * 256 + 256)
        for n in range(4):
            at = slice(n * 512, n * 512 + 512)
            value = m_ref[at, cols] + dot(xt[3, at, :], gv[h, 768:1024, :], NN) * f32(1.0 / 1024)
            m_ref[at, cols] = value
            high, low = split(value)
            wide = dot(high, bhl[...], NN)
            inner = wide[:, :128] + wide[:, 128:] + dot(low, bhl[:, :128], NN)
            cown[h, n * 8 : n * 8 + 8, :] = jnp.sum(inner.reshape(8, CH, 128) * bu4[...][None], axis=1)
        turned = cown[h].T
        own_ref[h, chip] = jnp.concatenate([turned[j * 32 : j * 32 + 32, :] for j in range(4)], axis=1)
        for dy, dz in offsets()[::-1]:
            send(h, own_ref, own_recv, chip, chip_at(dy, dz) * 2 + core)
            if h == 1:
                send(h, oth_ref, oth_recv, chip, chip_at(dy, dz) * 2 + 1 - core)
        send(h, oth_ref, oth_recv, chip, partner)

    outer(0, 8)
    momentum(0)
    forward(1)
    outer(8, 32)
    coefficients(0)
    momentum(1)
    coefficients(1)

    def take_away(h):
        for n in range(4):
            at, cols = slice(n * 512, n * 512 + 512), slice(h * 256, h * 256 + 256)
            field = cown[h, n * 8 : n * 8 + 8, :][:, None, :] * bu4[...][None]
            high, low = split(field.reshape(512, 128))
            back = dot(jnp.concatenate([high, low], axis=1), bhh[...], NT) + dot(high, bhl[:, 128:], NT)
            m_ref[at, cols] = m_ref[at, cols] - back

    rows = [pl.ds(pl.multiple_of(b * 256, 256), 256) for b in blocks]
    take_away(0)
    take_away(1)
    for cp in w_copies:
        cp.wait()
    input_grad(0, wv, gv, grad_ref, rows, 0)
    pass_on(0, 0, 15)
    fill(own_ref, 0, 0, sign_ref, lh, ll)
    acc[:, 0:512] = product(0, 0, 512, eh_ref, el_ref, lh, ll)
    acc[:, 512:1024] = product(1, 0, 512, eh_ref, el_ref, lh, ll)
    acc[:, 1024:1536] = product(2, 0, 512, eh_ref, el_ref, lh, ll)
    acc[:, 1536:2048] = product(3, 0, 512, eh_ref, el_ref, lh, ll)
    input_grad(1, wv, gv, grad_ref, rows, 1)
    for n in range(16):
        arrived(0, oth_ref, oth_recv, n)
    fill(oth_ref, 0, 1, sign_ref, lh, ll)
    for n in range(4):
        total = acc[:, n * 512 : n * 512 + 512] + product(n, 512, 1024, eh_ref, el_ref, lh, ll)
        place(0, n, total, wv, nw)
    for dy, dz in offsets():
        arrived(1, own_ref, own_recv, chip_at(-dy, -dz))
    for n in range(16):
        arrived(1, oth_ref, oth_recv, n)
    for cp in sends[0] + sends[1] + gone:
        cp.wait_send()


def input_grad(n, wv, gv, to, rows, place):
    part = None
    for h in range(2):
        pair = [wv[2 * h + k, n * 8 : n * 8 + 8].reshape(512, 128) for k in range(2)]
        high, low = split(jnp.concatenate(pair, axis=1))
        new = dot(gv[h], high, NT) + dot(gv[h], low, NT)
        part = new if part is None else part + new
    for s in range(4):
        to[rows[s], place * 512 : place * 512 + 512] = part[s * 256 : s * 256 + 256, :]


def fill(ref, h, half, sign_ref, lh, ll):
    at = slice(half * 512, half * 512 + 512)
    turned = ref[h].reshape(512, 128).T * f32(STEP_RATE)
    high, low = split(jnp.concatenate([turned, turned * sign_ref[0:1, at]], axis=0))
    lh[:, at] = high
    ll[:, at] = low


def product(n, first, last, eh_ref, el_ref, lh, ll):
    at, terms = slice(n * 512, n * 512 + 512), slice(first, last)
    high, low, eh = lh[:, terms], ll[:, terms], eh_ref[at, terms]
    return dot(high, eh, NT) + dot(low, eh, NT) + dot(high, el_ref[at, terms], NT)


def place(h, n, total, w_ref, nw):
    low_half = lax.broadcasted_iota(jnp.int32, (32, 128), 1) < 64
    for side in range(2):
        for j in range(2):
            vals = []
            for k in range(4):
                top = side * 128 + j * 64
                one = total[top : top + 32, k * 128 : k * 128 + 128]
                two = total[top + 32 : top + 64, k * 128 : k * 128 + 128]
                vals.append(jnp.where(low_half, one, pltpu.roll(two, 64, 1)))
                vals.append(jnp.where(low_half, pltpu.roll(one, 64, 1), two))
            first = 56 - 8 * n if side else 8 * n
            if side:
                vals = vals[::-1]
            rows = slice(first, first + 8)
            nw[j, :, rows, :] = w_ref[2 * h + j, :, rows, :] - jnp.swapaxes(jnp.stack(vals, axis=0), 0, 1)


def second_kernel(
    m_ref, grad_ref, eh_ref, el_ref, sign_ref, own_ref, oth_ref, new_ref, w_ref, gv,
    grad_hbm, res_hbm, new_hbm, rest, nw, lh, ll, sems,
):
    feat = lax.axis_index("feat")
    blocks = (feat, (feat + 3) % 4, (feat + 1) % 4, (feat + 2) % 4)
    rows = [pl.ds(pl.multiple_of(b * 256, 256), 256) for b in blocks]
    copies = []

    def start(src, dst):
        cp = pltpu.make_async_copy(src, dst, sems.at[len(copies)])
        cp.start()
        copies.append(cp)

    start(grad_ref, grad_hbm.at[:, pl.ds(0, 1024)])
    start(m_ref, res_hbm)
    for j in range(2):
        start(new_ref.at[j], new_hbm.at[:, :, pl.ds(j * 128, 128)])
    for n in range(2):
        input_grad(2 + n, w_ref, gv, rest, rows, n)
        start(rest.at[:, pl.ds(n * 512, 512)], grad_hbm.at[:, pl.ds(1024 + n * 512, 512)])
    fill(own_ref, 1, 0, sign_ref, lh, ll)
    fill(oth_ref, 1, 1, sign_ref, lh, ll)
    for n in range(4):
        place(1, n, product(n, 0, 1024, eh_ref, el_ref, lh, ll), w_ref, nw)
        for first in (8 * n, 56 - 8 * n):
            for j in range(2):
                part = pl.ds(first, 8)
                start(nw.at[j, :, part], new_hbm.at[:, part, pl.ds(256 + j * 128, 128)])
    for cp in copies:
        cp.wait()


def vmem(shape, dtype):
    return pltpu.VMEM(shape, dtype)


def body(x, g, w, mom, sel):
    any_space = pl.BlockSpec(memory_space=pl.ANY)
    vm = pl.BlockSpec(memory_space=pltpu.VMEM)
    mid = pl.pallas_call(
        first_kernel,
        out_shape=(
            vmem((2048, 512), f32),
            vmem((1024, 1024), f32),
            vmem((2048, 1024), bf16),
            vmem((2048, 1024), bf16),
            vmem((8, 1024), f32),
            vmem((2, 16, 32, 128), f32),
            vmem((2, 16, 32, 128), f32),
            vmem((2, 32, CH, 128), f32),
            vmem((4, 32, CH, 128), f32),
            vmem((2, 1024, 256), bf16),
        ),
        in_specs=[any_space] * 5,
        out_specs=[vm] * 10,
        scratch_shapes=[
            pltpu.VMEM((1024, 2048), bf16),
            pltpu.VMEM((4, 2048, 256), bf16),
            pltpu.VMEM((32, 32), jnp.int32),
            pltpu.VMEM((CH, 1024), f32),
            pltpu.VMEM((CH, 1024), f32),
            pltpu.VMEM((256, 256), bf16),
            pltpu.VMEM((256, 256), bf16),
            pltpu.VMEM((CH, 128), f32),
            pltpu.VMEM((2, 32, 128), f32),
            pltpu.VMEM((256, 1024), bf16),
            pltpu.VMEM((256, 1024), bf16),
            pltpu.VMEM((256, 2048), f32),
            pltpu.SemaphoreType.DMA((12,)),
            pltpu.SemaphoreType.DMA((12,)),
            pltpu.SemaphoreType.DMA((12,)),
            pltpu.SemaphoreType.DMA((62,)),
            pltpu.SemaphoreType.DMA((32,)),
            pltpu.SemaphoreType.DMA((32,)),
        ],
        compiler_params=pltpu.CompilerParams(
            collective_id=0, has_side_effects=True, vmem_limit_bytes=18 * MIB
        ),
        name="gather_and_select",
    )(*(pltpu.with_memory_space_constraint(v, pltpu.HBM) for v in (x, g, w.reshape(32, CH, 512), mom[0], sel)))
    grad, res, new = pl.pallas_call(
        second_kernel,
        out_shape=(
            jax.ShapeDtypeStruct((1024, 2048), f32),
            jax.ShapeDtypeStruct((2048, 512), f32),
            jax.ShapeDtypeStruct((32, CH, 512), f32),
        ),
        in_specs=[vm] * 10,
        out_specs=[any_space] * 3,
        scratch_shapes=[
            pltpu.VMEM((1024, 1024), f32),
            pltpu.VMEM((2, 32, CH, 128), f32),
            pltpu.VMEM((256, 1024), bf16),
            pltpu.VMEM((256, 1024), bf16),
            pltpu.SemaphoreType.DMA((22,)),
        ],
        compiler_params=pltpu.CompilerParams(vmem_limit_bytes=14 * MIB),
        name="decode_and_write",
    )(*(pltpu.with_memory_space_constraint(v, pltpu.VMEM) for v in mid))
    return grad, res[None], new.reshape(2048, 512)


def solution(mesh):
    in_specs = (P("rep", "feat"), P(("rep", "feat"), None), P("feat", None), P("rep", "feat", None), P())
    out_specs = (P("rep", "feat"), P("rep", "feat", None), P("feat", None))
    return jax.shard_map(body, mesh=mesh, in_specs=in_specs, out_specs=out_specs, check_vma=False)
```

```python
import functools

import jax
import jax.numpy as jnp
from jax import lax
from jax.experimental import pallas as pl
from jax.experimental.pallas import tpu as pltpu
from jax.sharding import PartitionSpec as P

CH = 64
MOMENTUM_DECAY = 0.9
STEP_RATE = 0.5
f32 = jnp.float32
bf16 = jnp.bfloat16
NN = (((1,), (0,)), ((), ()))
NT = (((1,), (1,)), ((), ()))
TN = (((0,), (0,)), ((), ()))
MIB = 1 << 20


def dot(a, b, dims, precision=None):
    return lax.dot_general(a, b, dims, precision=precision, preferred_element_type=f32)


def split(v):
    high = v.astype(bf16)
    return high, (v - high.astype(f32)).astype(bf16)


def dct_transposed():
    a = lax.broadcasted_iota(jnp.int32, (CH, CH), 0)
    u = lax.broadcasted_iota(jnp.int32, (CH, CH), 1)
    turn = ((2 * a + 1) * u) & 255
    table = jnp.cos(turn.astype(f32) * f32(jnp.pi / 128)) * f32((2.0 / CH) ** 0.5)
    return jnp.where(u == 0, f32((1.0 / CH) ** 0.5), table)


def pick(table, row):
    n = row.shape[1]
    hot = (lax.broadcasted_iota(jnp.int32, (CH, n), 0) == jnp.broadcast_to(row, (CH, n))).astype(f32)
    return dot(table, hot, NN, lax.Precision.HIGHEST)


def offsets():
    both = [(dy, dz) for dy in range(4) for dz in range(4) if (dy, dz) != (0, 0)]
    return sorted(both, key=lambda o: (min(o[0], 4 - o[0]) + min(o[1], 4 - o[1]), o))


def first_kernel(
    x_hbm, g_hbm, w_hbm, mom_hbm, sel_hbm,
    m_ref, grad_ref, eh_ref, el_ref, sign_ref, own_ref, oth_ref, nw, wv, gv, high_ref, low_ref,
    xv, xt, sel_ref, but, bvt, bhl, bhh, bu4, cown, lh, ll, acc,
    local_sem, g_send, g_recv, c_send, own_recv, oth_recv,
):
    feat = lax.axis_index("feat")
    rep = lax.axis_index("rep")
    core = rep % 2
    chip = rep // 2
    y, z = chip // 4, chip % 4
    partner = rep + 1 - 2 * core
    right, left, across = (feat + 1) % 4, (feat + 3) % 4, (feat + 2) % 4
    blocks = (feat, left, right, across)

    def chip_at(dy, dz):
        return (y + dy) % 4 * 4 + (z + dz) % 4

    barrier = pltpu.get_barrier_semaphore()
    for f in (left, right):
        pl.semaphore_signal(barrier, inc=1, device_id={"feat": f})
    for dy, dz in offsets():
        pl.semaphore_signal(barrier, inc=1, device_id={"rep": chip_at(dy, dz) * 2 + core})
        pl.semaphore_signal(barrier, inc=1, device_id={"rep": chip_at(dy, dz) * 2 + 1 - core})
    pl.semaphore_signal(barrier, inc=1, device_id={"rep": partner})

    sel_copy = pltpu.make_async_copy(sel_hbm, sel_ref, local_sem.at[0])
    own_g = [
        pltpu.make_async_copy(g_hbm.at[:, pl.ds(h * 256, 256)], gv.at[h, pl.ds(0, 256)], local_sem.at[1 + h])
        for h in range(2)
    ]
    x_copies = [
        pltpu.make_async_copy(x_hbm.at[pl.ds(b * 256, 256)], xv.at[pl.ds(n * 256, 256)], local_sem.at[3 + n])
        for n, b in enumerate(blocks)
    ]
    m_copy = pltpu.make_async_copy(mom_hbm, m_ref, local_sem.at[7])
    w_copies = [
        pltpu.make_async_copy(w_hbm.at[:, :, pl.ds(n * 128, 128)], wv.at[n], local_sem.at[8 + n]) for n in range(4)
    ]
    for cp in [sel_copy] + x_copies:
        cp.start()

    def g_copy(h, n, slot, half, to, forward=None):
        if forward is None:
            src = g_hbm.at[pl.ds(half * 128, 128), pl.ds(h * 256, 256)]
        else:
            src = gv.at[h, pl.ds(forward * 256 + half * 128, 128)]
        return pltpu.make_async_remote_copy(
            src_ref=src,
            dst_ref=gv.at[h, pl.ds(slot * 256 + half * 128, 128)],
            send_sem=g_send.at[h * 6 + n],
            recv_sem=g_recv.at[h * 6 + n],
            device_id={"feat": to},
        )

    sends = [
        [
            g_copy(h, 0, 1, 0, right),
            g_copy(h, 1, 2, 1, left),
            g_copy(h, 2, 1, 1, right),
            g_copy(h, 3, 2, 0, left),
            g_copy(h, 4, 3, 0, right, 1),
            g_copy(h, 5, 3, 1, left, 2),
        ]
        for h in range(2)
    ]
    pl.semaphore_wait(barrier, 33)
    for cp in sends[0][:4] + sends[1][:2]:
        cp.start()

    def forward(h):
        for n in range(2):
            sends[h][n].wait_recv()
            sends[h][4 + n].start()

    table = dct_transposed()
    sel_copy.wait()
    for cp in own_g + [m_copy]:
        cp.start()
    rows = []
    for s in range(32):
        plane = core if s < 16 else 1 - core
        rows.append(sel_ref[pl.ds((s % 16) * 2 + plane, 1), :])
    flat = jnp.concatenate(rows, axis=1)
    but[...] = pick(table, flat >> 6)
    bvt[...] = pick(table, flat & 63)
    sign_ref[...] = jnp.broadcast_to(f32(1) - f32(2) * ((flat >> 6) & 1).astype(f32), (8, 1024))
    mine = sel_ref[pl.ds(rep, 1), :]
    mine = jnp.concatenate([mine] * 4, axis=1)
    bu4[...] = pick(table, mine >> 6)
    tall = jnp.concatenate([pick(table, mine & 63)] * 4, axis=0)
    ahead = lax.broadcasted_iota(jnp.int32, (256, 128), 0) // 64
    along = lax.broadcasted_iota(jnp.int32, (256, 128), 1) // 32
    high, low = split(jnp.where(ahead == along, tall, f32(0)))
    bhl[:, :128] = high
    bhl[:, 128:] = low
    bhh[:, :128] = high
    bhh[:, 128:] = high

    for slot in range(4):
        x_copies[slot].wait()

        @pl.loop(0, 8)
        def _(n):
            at = pl.ds(pl.multiple_of(n * 256, 256), 256)
            xt[slot, at, :] = xv[slot * 256 : slot * 256 + 256, at].T

        if slot == 3:
            forward(0)
            for cp in sends[1][2:4] + w_copies:
                cp.start()

    def outer(first, last):
        @pl.loop(first, last)
        def _(a):
            high, low = split(but[pl.ds(a, 1), :] * bvt[...])
            to = pl.ds(pl.multiple_of(a * CH, CH), CH)
            eh_ref[to, :] = high
            el_ref[to, :] = low

    gone = []

    def send(h, dst, sem, at, to):
        cp = pltpu.make_async_remote_copy(
            src_ref=own_ref.at[h, at],
            dst_ref=dst.at[h, at],
            send_sem=c_send.at[len(gone)],
            recv_sem=sem.at[h * 16 + at],
            device_id={"rep": to},
        )
        cp.start()
        gone.append(cp)

    def arrived(h, ref, sem, at):
        pltpu.make_async_remote_copy(
            src_ref=ref.at[h, at], dst_ref=ref.at[h, at], send_sem=c_send.at[0], recv_sem=sem.at[h * 16 + at],
            device_id={"rep": partner},
        ).wait_recv()

    def pass_on(h, n0, n1):
        for dy, dz in offsets()[n0:n1]:
            at = chip_at(-dy, -dz)
            arrived(h, own_ref, own_recv, at)
            send(h, oth_ref, oth_recv, at, partner)

    def momentum(h):
        own_g[h].wait()
        sends[h][2].wait_recv()
        sends[h][3].wait_recv()
        if h == 0:
            m_copy.wait()
        cols = slice(h * 256, h * 256 + 256)
        for n in range(4):
            at = slice(n * 512, n * 512 + 512)
            lhs = jnp.concatenate([xt[s, at, :] for s in range(3)], axis=1)
            part = dot(lhs, gv[h, 0:768, :], NN) * f32(1.0 / 1024)
            m_ref[at, cols] = f32(MOMENTUM_DECAY) * m_ref[at, cols] + part

    def coefficients(h):
        sends[h][4].wait_recv()
        sends[h][5].wait_recv()
        cols = slice(h * 256, h * 256 + 256)
        for n in range(4):
            at = slice(n * 512, n * 512 + 512)
            value = m_ref[at, cols] + dot(xt[3, at, :], gv[h, 768:1024, :], NN) * f32(1.0 / 1024)
            m_ref[at, cols] = value
            high, low = split(value)
            wide = dot(high, bhl[...], NN)
            inner = wide[:, :128] + wide[:, 128:] + dot(low, bhl[:, :128], NN)
            cown[h, n * 8 : n * 8 + 8, :] = jnp.sum(inner.reshape(8, CH, 128) * bu4[...][None], axis=1)
        turned = cown[h].T
        own_ref[h, chip] = jnp.concatenate([turned[j * 32 : j * 32 + 32, :] for j in range(4)], axis=1)
        for dy, dz in offsets()[::-1]:
            send(h, own_ref, own_recv, chip, chip_at(dy, dz) * 2 + core)
            if h == 1:
                send(h, oth_ref, oth_recv, chip, chip_at(dy, dz) * 2 + 1 - core)
        send(h, oth_ref, oth_recv, chip, partner)

    def take_away(h):
        for n in range(4):
            at, cols = slice(n * 512, n * 512 + 512), slice(h * 256, h * 256 + 256)
            field = cown[h, n * 8 : n * 8 + 8, :][:, None, :] * bu4[...][None]
            high, low = split(field.reshape(512, 128))
            back = dot(jnp.concatenate([high, low], axis=1), bhh[...], NT) + dot(high, bhl[:, 128:], NT)
            m_ref[at, cols] = m_ref[at, cols] - back

    outer(0, 8)
    momentum(0)
    forward(1)
    outer(8, 32)
    coefficients(0)
    take_away(0)
    momentum(1)
    coefficients(1)

    rows = [pl.ds(pl.multiple_of(b * 256, 256), 256) for b in blocks]
    take_away(1)
    for cp in w_copies:
        cp.wait()
    input_grad(0, wv, gv, grad_ref, rows, 0)
    pass_on(0, 0, 15)
    fill(own_ref, 0, 0, sign_ref, lh, ll)
    acc[:, 0:512] = product(0, 0, 512, eh_ref, el_ref, lh, ll)
    acc[:, 512:1024] = product(1, 0, 512, eh_ref, el_ref, lh, ll)
    acc[:, 1024:1536] = product(2, 0, 512, eh_ref, el_ref, lh, ll)
    acc[:, 1536:2048] = product(3, 0, 512, eh_ref, el_ref, lh, ll)
    input_grad(1, wv, gv, grad_ref, rows, 1)
    for n in range(16):
        arrived(0, oth_ref, oth_recv, n)
    fill(oth_ref, 0, 1, sign_ref, lh, ll)
    for n in range(4):
        total = acc[:, n * 512 : n * 512 + 512] + product(n, 512, 1024, eh_ref, el_ref, lh, ll)
        place(0, n, total, wv, nw)
    for dy, dz in offsets():
        arrived(1, own_ref, own_recv, chip_at(-dy, -dz))
    fill(own_ref, 1, 0, sign_ref, high_ref, low_ref)
    for n in range(16):
        arrived(1, oth_ref, oth_recv, n)
    for cp in sends[0] + sends[1] + gone:
        cp.wait_send()


def input_grad(n, wv, gv, to, rows, place):
    part = None
    for h in range(2):
        pair = [wv[2 * h + k, n * 8 : n * 8 + 8].reshape(512, 128) for k in range(2)]
        high, low = split(jnp.concatenate(pair, axis=1))
        new = dot(gv[h], high, NT) + dot(gv[h], low, NT)
        part = new if part is None else part + new
    for s in range(4):
        to[rows[s], place * 512 : place * 512 + 512] = part[s * 256 : s * 256 + 256, :]


def fill(ref, h, half, sign_ref, lh, ll):
    at = slice(half * 512, half * 512 + 512)
    turned = ref[h].reshape(512, 128).T * f32(STEP_RATE)
    high, low = split(jnp.concatenate([turned, turned * sign_ref[0:1, at]], axis=0))
    lh[:, at] = high
    ll[:, at] = low


def product(n, first, last, eh_ref, el_ref, lh, ll):
    at, terms = slice(n * 512, n * 512 + 512), slice(first, last)
    high, low, eh = lh[:, terms], ll[:, terms], eh_ref[at, terms]
    return dot(high, eh, NT) + dot(low, eh, NT) + dot(high, el_ref[at, terms], NT)


def place(h, n, total, w_ref, nw):
    low_half = lax.broadcasted_iota(jnp.int32, (32, 128), 1) < 64
    for side in range(2):
        for j in range(2):
            vals = []
            for k in range(4):
                top = side * 128 + j * 64
                one = total[top : top + 32, k * 128 : k * 128 + 128]
                two = total[top + 32 : top + 64, k * 128 : k * 128 + 128]
                vals.append(jnp.where(low_half, one, pltpu.roll(two, 64, 1)))
                vals.append(jnp.where(low_half, pltpu.roll(one, 64, 1), two))
            first = 56 - 8 * n if side else 8 * n
            if side:
                vals = vals[::-1]
            rows = slice(first, first + 8)
            nw[j, :, rows, :] = w_ref[2 * h + j, :, rows, :] - jnp.swapaxes(jnp.stack(vals, axis=0), 0, 1)


def second_kernel(
    m_ref, grad_ref, eh_ref, el_ref, sign_ref, own_ref, oth_ref, new_ref, w_ref, gv, high_ref, low_ref,
    grad_hbm, res_hbm, new_hbm, rest, nw, lh, ll, sems,
):
    feat = lax.axis_index("feat")
    blocks = (feat, (feat + 3) % 4, (feat + 1) % 4, (feat + 2) % 4)
    rows = [pl.ds(pl.multiple_of(b * 256, 256), 256) for b in blocks]
    copies = []

    def start(src, dst):
        cp = pltpu.make_async_copy(src, dst, sems.at[len(copies)])
        cp.start()
        copies.append(cp)

    start(grad_ref, grad_hbm.at[:, pl.ds(0, 1024)])
    start(m_ref, res_hbm)
    for j in range(2):
        start(new_ref.at[j], new_hbm.at[:, :, pl.ds(j * 128, 128)])
    for n in range(2):
        input_grad(2 + n, w_ref, gv, rest, rows, n)
        start(rest.at[:, pl.ds(n * 512, 512)], grad_hbm.at[:, pl.ds(1024 + n * 512, 512)])
    lh[:, 0:512] = high_ref[...]
    ll[:, 0:512] = low_ref[...]
    fill(oth_ref, 1, 1, sign_ref, lh, ll)
    for n in range(4):
        place(1, n, product(n, 0, 1024, eh_ref, el_ref, lh, ll), w_ref, nw)
        for first in (8 * n, 56 - 8 * n):
            for j in range(2):
                part = pl.ds(first, 8)
                start(nw.at[j, :, part], new_hbm.at[:, part, pl.ds(256 + j * 128, 128)])
    for cp in copies:
        cp.wait()


def vmem(shape, dtype):
    return pltpu.VMEM(shape, dtype)


def body(x, g, w, mom, sel):
    any_space = pl.BlockSpec(memory_space=pl.ANY)
    vm = pl.BlockSpec(memory_space=pltpu.VMEM)
    mid = pl.pallas_call(
        first_kernel,
        out_shape=(
            vmem((2048, 512), f32),
            vmem((1024, 1024), f32),
            vmem((2048, 1024), bf16),
            vmem((2048, 1024), bf16),
            vmem((8, 1024), f32),
            vmem((2, 16, 32, 128), f32),
            vmem((2, 16, 32, 128), f32),
            vmem((2, 32, CH, 128), f32),
            vmem((4, 32, CH, 128), f32),
            vmem((2, 1024, 256), bf16),
            vmem((256, 512), bf16),
            vmem((256, 512), bf16),
        ),
        in_specs=[any_space] * 5,
        out_specs=[vm] * 12,
        scratch_shapes=[
            pltpu.VMEM((1024, 2048), bf16),
            pltpu.VMEM((4, 2048, 256), bf16),
            pltpu.VMEM((32, 32), jnp.int32),
            pltpu.VMEM((CH, 1024), f32),
            pltpu.VMEM((CH, 1024), f32),
            pltpu.VMEM((256, 256), bf16),
            pltpu.VMEM((256, 256), bf16),
            pltpu.VMEM((CH, 128), f32),
            pltpu.VMEM((2, 32, 128), f32),
            pltpu.VMEM((256, 1024), bf16),
            pltpu.VMEM((256, 1024), bf16),
            pltpu.VMEM((256, 2048), f32),
            pltpu.SemaphoreType.DMA((12,)),
            pltpu.SemaphoreType.DMA((12,)),
            pltpu.SemaphoreType.DMA((12,)),
            pltpu.SemaphoreType.DMA((62,)),
            pltpu.SemaphoreType.DMA((32,)),
            pltpu.SemaphoreType.DMA((32,)),
        ],
        compiler_params=pltpu.CompilerParams(
            collective_id=0, has_side_effects=True, vmem_limit_bytes=18 * MIB
        ),
        name="gather_and_select",
    )(*(pltpu.with_memory_space_constraint(v, pltpu.HBM) for v in (x, g, w.reshape(32, CH, 512), mom[0], sel)))
    grad, res, new = pl.pallas_call(
        second_kernel,
        out_shape=(
            jax.ShapeDtypeStruct((1024, 2048), f32),
            jax.ShapeDtypeStruct((2048, 512), f32),
            jax.ShapeDtypeStruct((32, CH, 512), f32),
        ),
        in_specs=[vm] * 12,
        out_specs=[any_space] * 3,
        scratch_shapes=[
            pltpu.VMEM((1024, 1024), f32),
            pltpu.VMEM((2, 32, CH, 128), f32),
            pltpu.VMEM((256, 1024), bf16),
            pltpu.VMEM((256, 1024), bf16),
            pltpu.SemaphoreType.DMA((22,)),
        ],
        compiler_params=pltpu.CompilerParams(vmem_limit_bytes=14 * MIB),
        name="decode_and_write",
    )(*(pltpu.with_memory_space_constraint(v, pltpu.VMEM) for v in mid))
    return grad, res[None], new.reshape(2048, 512)


def solution(mesh):
    in_specs = (P("rep", "feat"), P(("rep", "feat"), None), P("feat", None), P("rep", "feat", None), P())
    out_specs = (P("rep", "feat"), P("rep", "feat", None), P("feat", None))
    return jax.shard_map(body, mesh=mesh, in_specs=in_specs, out_specs=out_specs, check_vma=False)
```
